256 devices in a mesh: clip: 64 (over x, z, core), cap: 4 (over y).
Axes of the slice: x: 4, y: 4, z: 8, core: 2. Of those that a mesh axis runs over, the one named last changes fastest.
Arguments:
- text: bfloat16 [1024, 512], replicated, may hold values from -8 to 8
- patches: bfloat16 [128, 16, 196, 512], P('clip', None, 'cap'), may hold values from -6 to 6
- frame_slots: int32 [128, 16], P('clip'), may hold values from -1 to 1023, as said below
Outputs:
- contrast_loss: float32 [], replicated
- patch_grad: bfloat16 [128, 16, 196, 512], P('clip', None, 'cap')
- text_grad: float32 [1024, 512], P(('clip', 'cap'))
The draws below stay inside these ranges and needn't reach their ends.
Inputs may be any that keep to these rules, and one draw needn't show every extreme that they name: `frame_slots`: in every clip the valid frames are the first 4 to 16 slots, and on some index of clip every clip has all 16; all clips together have 128 * 8 valid frames. A valid entry is t * 16 + s: the frame goes to index t of clip, slot s; every index of clip receives exactly 16 frames, one in each slot. A frame stays on its own index of clip unless that index holds more than 16 frames; then its frames past the first 16, in clip and frame order, go to other indices. At most 2 frames go from one index of clip to another, a bound that some pair reaches.
All inputs are finite; a program needn't handle non-finite values.
Results may differ from the reference program's by a relative error of at most 0.0065.
Values may be sent and summed in bfloat16 or wider, within the bound.
A program may use at most 64 MiB of HBM per device.

```python
import jax
import jax.numpy as jnp
from jax import lax

D = 512
PATCHES = 196
WORDS = 8
FMAX = 16
MEANF = 8
CLIP_DEV = 2
CLIPS = 128
SLOTS = 16


def draw_text(key, part):
    values = jax.random.truncated_normal(jax.random.fold_in(key, 1), -4.0, 4.0, (CLIPS * WORDS, D), jnp.float32)
    return values.astype(jnp.bfloat16)


def draw_patches(key, part):
    values = jax.random.truncated_normal(jax.random.fold_in(key, 3), -4.0, 4.0, (CLIPS, FMAX, PATCHES, D), jnp.float32)
    return values.astype(jnp.bfloat16)


def fill_greedy(total, proposed, ceiling):
    before = jnp.cumsum(proposed) - proposed
    first_pass = jnp.clip(total - before, 0, proposed)
    leftover = total - jnp.sum(first_pass)
    headroom = ceiling - first_pass
    before_room = jnp.cumsum(headroom) - headroom
    second_pass = jnp.clip(leftover - before_room, 0, headroom)
    return first_pass + second_pass


def draw_frame_slots(key, part):
    subkeys = jax.random.split(jax.random.fold_in(key, 57), 6)
    devices = CLIPS // CLIP_DEV
    excess = CLIP_DEV * (FMAX - MEANF)
    room_most = max(2, (excess + devices - 2) // (devices - 1))
    device_index = jnp.arange(devices, dtype=jnp.int32)
    full_device = jax.random.randint(subkeys[0], (), 0, devices)
    empty_device = (full_device + 1 + jax.random.randint(subkeys[1], (), 0, devices - 1)) % devices
    is_full = device_index == full_device
    is_empty = device_index == empty_device
    others = jnp.logical_not(is_full | is_empty).astype(jnp.int32)
    extra = (devices - 1) * room_most - excess
    shuffle = jax.random.permutation(subkeys[2], devices)
    proposed_add = jax.random.randint(subkeys[3], (devices,), 0, room_most + 1) * others
    added_order = fill_greedy(extra, proposed_add[shuffle], room_most * others[shuffle])
    added = jnp.zeros((devices,), jnp.int32).at[shuffle].set(added_order)
    totals = jnp.where(is_full, CLIP_DEV * FMAX, SLOTS - room_most + added)
    clip_extra = jax.random.randint(subkeys[4], (devices, CLIP_DEV), 0, FMAX - 3)
    split = jax.vmap(fill_greedy, in_axes=(0, 0, None))(totals - 4 * CLIP_DEV, clip_extra, FMAX - 4)
    frames = (4 + split).reshape(CLIPS)
    present = jnp.arange(FMAX, dtype=jnp.int32)[None, :] < frames[:, None]
    ranks = jnp.cumsum(present.reshape(devices, CLIP_DEV * FMAX).astype(jnp.int32), axis=1) - 1
    ranks = ranks.reshape(CLIPS, FMAX)
    owner = (jnp.arange(CLIPS, dtype=jnp.int32) // CLIP_DEV)[:, None]
    home = ranks < SLOTS
    room = SLOTS - jnp.minimum(totals, SLOTS)
    mixing = jax.random.permutation(subkeys[5], devices)
    place = jnp.zeros((devices,), jnp.int32).at[mixing].set(device_index)
    receive_order = jnp.argsort(jnp.where(is_empty, -1, place), stable=True)
    room_ordered = room[receive_order]
    start_ordered = jnp.cumsum(room_ordered) - room_ordered
    room_start = jnp.zeros((devices,), jnp.int32).at[receive_order].set(start_ordered)
    beyond = ranks - SLOTS
    hit = (beyond[:, :, None] >= room_start[None, None, :]) & (beyond[:, :, None] < (room_start + room)[None, None, :])
    receiver = jnp.sum(jnp.where(hit, device_index[None, None, :], 0), axis=2)
    far_slot = totals[receiver] + beyond - room_start[receiver]
    target = jnp.where(home, owner, receiver)
    slot = jnp.where(home, ranks, far_slot)
    return jnp.where(present, target * SLOTS + slot, -1)


def setup_inputs(seed: int = 0) -> dict:
    arg_keys = jax.random.split(jax.random.key(seed), 4)
    text = draw_text(jax.random.fold_in(arg_keys[3], 71), 0)
    patches = draw_patches(jax.random.fold_in(arg_keys[3], 71), 0)
    frame_slots = draw_frame_slots(jax.random.fold_in(arg_keys[3], 71), 0)
    return dict(text=text, patches=patches, frame_slots=frame_slots)


logit_scale = 32.0
loss_scale = 8192.0
big_value = 1e30


def frame_scores(text, frames):
    flattened = frames.reshape(-1, frames.shape[-1])
    scores = lax.dot_general(text, flattened, (((1,), (1,)), ((), ())), preferred_element_type=jnp.float32)
    return scores * (D ** -0.5)


def usable_columns(slot_row):
    return jnp.repeat(slot_row >= 0, PATCHES)[None, :]


def pool_clip(text, frames, slot_row):
    scores = frame_scores(text, frames)
    usable = usable_columns(slot_row)
    maximum = jnp.max(jnp.where(usable, scores, -big_value), axis=1)
    weight = jnp.where(usable, jnp.exp(scores - maximum[:, None]), 0.0)
    totals = jnp.sum(weight, axis=1)
    pooled = jnp.sum(weight * scores, axis=1) / totals
    return maximum, totals, pooled


def reference(text, patches, frame_slots):
    maxima, sums, pooled = lax.map(lambda element: pool_clip(text, element[0], element[1]), (patches, frame_slots))
    similar = jnp.mean(pooled.reshape(CLIPS, CLIPS, WORDS), axis=2)
    logits = logit_scale * similar.T
    row_terms = jax.nn.logsumexp(logits, axis=1)
    col_terms = jax.nn.logsumexp(logits, axis=0)
    matched = jnp.diagonal(logits)
    contrast_loss = 0.5 * (jnp.mean(row_terms - matched) + jnp.mean(col_terms - matched))
    identity = jnp.eye(CLIPS, dtype=logits.dtype)
    grad_logits = (loss_scale * 0.5 / CLIPS) * (jax.nn.softmax(logits, axis=1) + jax.nn.softmax(logits, axis=0) - 2.0 * identity)
    grad_pooled = jnp.repeat((logit_scale / WORDS) * grad_logits.T, WORDS, axis=1)

    def backward(running, element):
        frames, slot_row, maximum, totals, pool_row, grad_row = element
        scores = frame_scores(text, frames)
        usable = usable_columns(slot_row)
        weights = jnp.where(usable, jnp.exp(scores - maximum[:, None]) / totals[:, None], 0.0)
        grad_scores = (grad_row[:, None] * weights * (1.0 + scores - pool_row[:, None])).astype(jnp.bfloat16)
        grad_frames = lax.dot_general(grad_scores, text, (((0,), (0,)), ((), ())), preferred_element_type=jnp.float32) * (D ** -0.5)
        flattened = frames.reshape(-1, frames.shape[-1])
        running = running + lax.dot_general(grad_scores, flattened, (((1,), (0,)), ((), ())), preferred_element_type=jnp.float32) * (D ** -0.5)
        return running, grad_frames.astype(jnp.bfloat16).reshape(frames.shape)

    text_grad, patch_grad = lax.scan(backward, jnp.zeros(text.shape, jnp.float32), (patches, frame_slots, maxima, sums, pooled, grad_pooled))
    return contrast_loss, patch_grad, text_grad
```

```python
import jax
import jax.numpy as jnp
from jax import lax
from jax.experimental import pallas as pl
from jax.experimental.pallas import tpu as pltpu
from jax.sharding import Mesh
from jax.sharding import PartitionSpec as P

XS, ZS, CS, YS = 4, 8, 2, 4
WORDS = 8
ROWS = 1024
DIM = 512
FRAMES = 16
PATCH = 49
CLIP_ROWS = FRAMES * PATCH
CAPS = 128
CHUNK = 256
HALF = 512
BLOCK = 128
SCALE = DIM**-0.5
LOG2E = 1.4426950408889634
LN2 = 0.6931471805599453
BIG = 1e30
LOGIT_SCALE = 32.0
LOSS_SCALE = 8192.0
NT = (((1,), (1,)), ((), ()))
NN = (((1,), (0,)), ((), ()))


def mm(a, b, dims):
    return lax.dot_general(a, b, dims, preferred_element_type=jnp.float32)


def three_parts(value):
    first = value.astype(jnp.bfloat16)
    rest = value - first.astype(jnp.float32)
    second = rest.astype(jnp.bfloat16)
    third = (rest - second.astype(jnp.float32)).astype(jnp.bfloat16)
    return jnp.concatenate([first, second, third], axis=0)


def added_parts(value, rows):
    return value[:rows] + value[rows : 2 * rows] + value[2 * rows : 3 * rows]


def kernel(
    text_hbm, patch_hbm, slots_ref,
    loss_ref, pg_ref, tg_ref,
    text_in, text_wide, text_perm, patch, patch_t, bias_ref, member,
    z_ref, gh_ref, cap_rx, near_rx, far_rx,
    t_own, t_send, t_recv, coef_ref,
    snd1, own1, rcv1, snd2, own2, rcv2, sum2, snd3, own3, rcv3, pg_buf, gs_ref,
    text_sem, patch_sem, pg_sem,
    cap_ss, cap_rs, near_ss, near_rs, far_ss, far_rs, core_ss, core_rs,
    ss1, rs1, ss2, rs2, ss3, rs3,
):
    x = lax.axis_index("x")
    z = lax.axis_index("z")
    core = lax.axis_index("core")
    y = lax.axis_index("y")
    xc = x * CS + core

    text_copy = pltpu.make_async_copy(text_hbm, text_in, text_sem)
    text_copy.start()
    patch_copies = []
    for v in range(2):
        rows = pl.ds(v * CLIP_ROWS, CLIP_ROWS)
        copy = pltpu.make_async_copy(patch_hbm.at[rows], patch.at[rows], patch_sem.at[v])
        copy.start()
        patch_copies.append(copy)

    def near_peer(i):
        other = lax.rem(xc + i, XS * CS)
        return (other // CS, z, lax.rem(other, CS), y)

    def far_peer(i):
        return (x, lax.rem(z + i, ZS), core, y)

    def cap_peer(i):
        return (x, z, core, lax.rem(y + i, YS))

    barrier = pltpu.get_barrier_semaphore()
    peers = [near_peer(i) for i in range(1, XS * CS)]
    peers += [far_peer(i) for i in range(1, ZS)]
    peers += [cap_peer(i) for i in range(1, YS)]
    for peer in peers:
        pl.semaphore_signal(barrier, inc=1, device_id=peer, device_id_type=pl.DeviceIdType.MESH)

    slots = slots_ref[...]
    at_row = lax.broadcasted_iota(jnp.int32, (FRAMES, FRAMES), 0)
    at_col = lax.broadcasted_iota(jnp.int32, (FRAMES, FRAMES), 1)
    for v in range(2):
        usable = jnp.where(slots[v : v + 1] >= 0, 0.0, -BIG)
        spread = jnp.where(at_row == at_col, jnp.broadcast_to(usable, (FRAMES, FRAMES)), 0.0)
        column = jnp.sum(spread, axis=1, keepdims=True)
        bias_ref[v] = jnp.broadcast_to(column, (FRAMES, BLOCK))

    q = lax.broadcasted_iota(jnp.int32, (ROWS, CAPS), 0)
    c = lax.broadcasted_iota(jnp.int32, (ROWS, CAPS), 1)
    qh, q1, q2, qz = q // 512, (q // 128) % 4, (q // 8) % 4, q % 8
    qy = jnp.where(qh == 0, q1, q2)
    qx = jnp.where(qh == 0, q2, q1)
    caption = qx * 32 + qz * 4 + qh * 2 + qy // 2
    member[...] = jnp.where(caption == c, 1.0, 0.0).astype(jnp.bfloat16)

    text_copy.wait()
    for j in range(4):
        text_wide[j] = text_in[:, j * BLOCK : (j + 1) * BLOCK].astype(jnp.float32)
    for h in range(2):
        for b1 in range(4):
            for k in range(4):
                base = h * 512 + b1 * 128 + k * 32
                for j in range(4):
                    pieces = []
                    for b2 in range(4):
                        fx, fy = (b2, b1) if h == 0 else (b1, b2)
                        start = fx * 256 + h * 16 + fy * 4 + k
                        pieces.append(text_wide[j, pl.ds(start, 8, stride=32), :])
                    group = jnp.concatenate(pieces, axis=0).astype(jnp.bfloat16)
                    text_perm[base : base + 32, j * BLOCK : (j + 1) * BLOCK] = group

    def tiled(value):
        return jnp.broadcast_to(value, (FRAMES, CHUNK))

    def wide_bias(v):
        part = bias_ref[v]
        return jnp.concatenate([part, part], axis=1)

    def forward(i, _):
        v, n = i // 4, i % 4
        scores = mm(
            patch[pl.ds(pl.multiple_of(v * CLIP_ROWS, 16), CLIP_ROWS), :],
            text_perm[pl.ds(pl.multiple_of(n * CHUNK, CHUNK), CHUNK), :],
            NT,
        )
        z_ref[i] = scores
        top = z_ref[i, 0:FRAMES, :]
        for p in range(1, PATCH):
            top = jnp.maximum(top, z_ref[i, p * FRAMES : (p + 1) * FRAMES, :])
        bias = wide_bias(v)
        peak = jnp.max(top + bias, axis=0, keepdims=True) * (SCALE * LOG2E)
        offset = bias - tiled(peak)
        total = jnp.zeros((FRAMES, CHUNK), jnp.float32)
        weighted = jnp.zeros((FRAMES, CHUNK), jnp.float32)
        for p in range(PATCH):
            s = z_ref[i, p * FRAMES : (p + 1) * FRAMES, :]
            e = jnp.exp2(s * (SCALE * LOG2E) + offset)
            total = total + e
            weighted = weighted + e * s
        total = jnp.sum(total, axis=0, keepdims=True)
        weighted = jnp.sum(weighted, axis=0, keepdims=True)
        lanes = pl.ds(pl.multiple_of(n * CHUNK, CHUNK), CHUNK)
        cap_rx[y, v, 0:1, lanes] = peak + jnp.log(total) * LOG2E
        cap_rx[y, v, 1:2, lanes] = weighted * SCALE / total
        return 0

    patch_copies[0].wait()
    patch_copies[1].wait()
    lax.fori_loop(0, 8, forward, 0)

    pl.semaphore_wait(barrier, len(peers))

    cap_copies = []
    for i in range(1, YS):
        copy = pltpu.make_async_remote_copy(
            src_ref=cap_rx.at[y], dst_ref=cap_rx.at[y],
            send_sem=cap_ss.at[i - 1], recv_sem=cap_rs.at[i - 1],
            device_id=cap_peer(i), device_id_type=pl.DeviceIdType.MESH,
        )
        copy.start()
        cap_copies.append(copy)

    for v in range(2):
        patch_t[v] = patch[v * CLIP_ROWS : (v + 1) * CLIP_ROWS, :].T

    for copy in cap_copies:
        copy.wait()

    lse, pooled = [], []
    for v in range(2):
        parts = [cap_rx[j, v, 0:1, :] for j in range(YS)]
        top = jnp.maximum(jnp.maximum(parts[0], parts[1]), jnp.maximum(parts[2], parts[3]))
        factors = [jnp.exp2(part - top) for part in parts]
        total = factors[0] + factors[1] + factors[2] + factors[3]
        mean = factors[0] * cap_rx[0, v, 1:2, :]
        for j in range(1, YS):
            mean = mean + factors[j] * cap_rx[j, v, 1:2, :]
        pooled.append(mean / total)
        lse.append(top + jnp.log(total) * LOG2E)
    both = jnp.concatenate(pooled, axis=0)
    logits_own = added_parts(mm(three_parts(both), member[...], NN), 2) * (LOGIT_SCALE / WORDS)
    near_rx[xc] = logits_own
    near_copies = []
    for i in range(1, XS * CS):
        copy = pltpu.make_async_remote_copy(
            src_ref=near_rx.at[xc], dst_ref=near_rx.at[xc],
            send_sem=near_ss.at[i - 1], recv_sem=near_rs.at[i - 1],
            device_id=near_peer(i), device_id_type=pl.DeviceIdType.MESH,
        )
        copy.start()
        near_copies.append(copy)

    for v in range(2):
        cap_rx[y, v, 0:1, :] = lse[v]
        cap_rx[y, v, 1:2, :] = 1.0 - pooled[v]

    def shaped(half):
        def body(i, _):
            v, m = i // 2, i % 2
            n = half * 2 + m
            lanes = pl.ds(pl.multiple_of(n * CHUNK, CHUNK), CHUNK)
            offset = wide_bias(v) - tiled(cap_rx[y, v, 0:1, lanes])
            shift = tiled(cap_rx[y, v, 1:2, lanes])
            inner = pl.ds(pl.multiple_of(m * CHUNK, CHUNK), CHUNK)
            j = v * 4 + n
            for p in range(PATCH):
                s = z_ref[j, p * FRAMES : (p + 1) * FRAMES, :]
                w = jnp.exp2(s * (SCALE * LOG2E) + offset)
                g = w * (s * SCALE + shift)
                gh_ref[v, half, p * FRAMES : (p + 1) * FRAMES, inner] = g.astype(jnp.bfloat16)
            return 0

        lax.fori_loop(0, 4, body, 0)

    other = 1 - core
    shaped(other)
    core_copies = []
    for v in range(2):
        t_send[v] = mm(patch_t[v], gh_ref[v, other], NN).astype(jnp.bfloat16)
        copy = pltpu.make_async_remote_copy(
            src_ref=t_send.at[v], dst_ref=t_recv.at[v],
            send_sem=core_ss.at[v], recv_sem=core_rs.at[v],
            device_id=(x, z, other, y), device_id_type=pl.DeviceIdType.MESH,
        )
        copy.start()
        core_copies.append(copy)

    for copy in near_copies:
        copy.wait()
    far_rx[z] = jnp.concatenate([near_rx[j] for j in range(XS * CS)], axis=0)
    far_copies = []
    for i in range(1, ZS):
        copy = pltpu.make_async_remote_copy(
            src_ref=far_rx.at[z], dst_ref=far_rx.at[z],
            send_sem=far_ss.at[i - 1], recv_sem=far_rs.at[i - 1],
            device_id=far_peer(i), device_id_type=pl.DeviceIdType.MESH,
        )
        copy.start()
        far_copies.append(copy)

    shaped(core)
    for v in range(2):
        t_own[v] = mm(patch_t[v], gh_ref[v, core], NN)

    for copy in far_copies:
        copy.wait()

    logits = jnp.concatenate([far_rx[j] for j in range(ZS)], axis=0)
    row = lax.broadcasted_iota(jnp.int32, (CAPS, CAPS), 0)
    col = lax.broadcasted_iota(jnp.int32, (CAPS, CAPS), 1)
    clip = ((row // 4) % 4) * 32 + (row // 16) * 4 + row % 4
    matched = jnp.sum(jnp.where(clip == col, logits, 0.0), axis=1, keepdims=True)
    cap_top = jnp.max(logits, axis=0, keepdims=True)
    cap_lse = cap_top + jnp.log(jnp.sum(jnp.exp(logits - cap_top), axis=0, keepdims=True))
    clip_top = jnp.max(logits, axis=1, keepdims=True)
    clip_lse = clip_top + jnp.log(jnp.sum(jnp.exp(logits - clip_top), axis=1, keepdims=True))
    terms = jnp.sum(cap_lse, axis=1, keepdims=True) + jnp.sum(clip_lse - 2.0 * matched, axis=0, keepdims=True)
    loss_ref[...] = terms * (0.5 / CAPS)

    near = jnp.concatenate([near_rx[xc], near_rx[x * CS + other]], axis=0)
    near_top = jnp.max(near, axis=1, keepdims=True)
    near_exp = jnp.exp(near - near_top)
    by_clip = near_exp / jnp.sum(near_exp, axis=1, keepdims=True)
    by_cap = jnp.exp(near - cap_lse)
    row = lax.broadcasted_iota(jnp.int32, (4, CAPS), 0)
    col = lax.broadcasted_iota(jnp.int32, (4, CAPS), 1)
    which = jnp.where(row < 2, core, other)
    mine = (x * ZS + z) * 4 + which * 2 + row % 2
    eye = jnp.where(mine == col, 1.0, 0.0)
    grad = (by_clip + by_cap - 2.0 * eye) * (LOSS_SCALE * 0.5 / CAPS * LOGIT_SCALE / WORDS * SCALE)
    coef = added_parts(mm(three_parts(grad), member[...], NT), 4)
    coef_ref[0] = coef[:, :HALF]
    coef_ref[1] = coef[:, HALF:]

    for copy in core_copies:
        copy.wait()

    first = y + core * (x - y)
    second = x + core * (y - x)

    def first_peer(b):
        return (x + core * (b - x), z, core, b + core * (y - b))

    def second_peer(b):
        return (b + core * (x - b), z, core, y + core * (b - y))

    copies1 = []
    for slot, i in enumerate((2, 1, 3, 0)):
        b = lax.rem(first + i, 4)
        lanes = pl.ds(pl.multiple_of(b * BLOCK, BLOCK), BLOCK)
        part = coef_ref[core, 0:1, lanes] * t_own[0, :, lanes]
        part = part + coef_ref[core, 1:2, lanes] * t_own[1, :, lanes]
        part = part + coef_ref[core, 2:3, lanes] * t_recv[0, :, lanes].astype(jnp.float32)
        part = part + coef_ref[core, 3:4, lanes] * t_recv[1, :, lanes].astype(jnp.float32)
        if i == 0:
            own1[...] = part
        else:
            snd1[slot] = part.astype(jnp.bfloat16)
            copy = pltpu.make_async_remote_copy(
                src_ref=snd1.at[slot], dst_ref=rcv1.at[slot],
                send_sem=ss1.at[slot], recv_sem=rs1.at[slot],
                device_id=first_peer(b), device_id_type=pl.DeviceIdType.MESH,
            )
            copy.start()
            copies1.append(copy)

    pg_copies = []
    for v in range(2):
        def scaled(p, _, v=v):
            rows = pl.ds(pl.multiple_of(p * 112, 16), 112)
            for h in range(2):
                g = gh_ref[v, h, rows, :].astype(jnp.float32) * coef_ref[h, v : v + 1, :]
                gs_ref[rows, h * HALF : (h + 1) * HALF] = g.astype(jnp.bfloat16)
            return 0

        lax.fori_loop(0, 7, scaled, 0)
        rows = pl.ds(v * CLIP_ROWS, CLIP_ROWS)
        pg_buf[rows, :] = mm(gs_ref[...], text_perm[...], NN).astype(jnp.bfloat16)
        copy = pltpu.make_async_copy(pg_buf.at[rows], pg_ref.at[rows], pg_sem.at[v])
        copy.start()
        pg_copies.append(copy)

    for copy in copies1:
        copy.wait()
    summed = own1[...]
    for slot in range(3):
        summed = summed + rcv1[slot].astype(jnp.float32)
    own2[...] = summed.T
    copies2 = []
    for slot, i in enumerate((2, 1, 3)):
        b = lax.rem(second + i, 4)
        part = jnp.concatenate(
            [own2[pl.ds(pl.multiple_of(k * 32 + b * 8, 8), 8), :] for k in range(4)], axis=0
        )
        snd2[slot] = part.astype(jnp.bfloat16)
        copy = pltpu.make_async_remote_copy(
            src_ref=snd2.at[slot], dst_ref=rcv2.at[slot],
            send_sem=ss2.at[slot], recv_sem=rs2.at[slot],
            device_id=second_peer(b), device_id_type=pl.DeviceIdType.MESH,
        )
        copy.start()
        copies2.append(copy)
    summed = jnp.concatenate(
        [own2[pl.ds(pl.multiple_of(k * 32 + second * 8, 8), 8), :] for k in range(4)], axis=0
    )
    for copy in copies2:
        copy.wait()
    for slot in range(3):
        summed = summed + rcv2[slot].astype(jnp.float32)
    for m in range(4):
        sum2[m] = summed[:, m * BLOCK : (m + 1) * BLOCK]
    for j in range(ZS):
        part = jnp.concatenate([sum2[m, pl.ds(j, 4, stride=8), :] for m in range(4)], axis=1)
        own3[j] = part
        snd3[j] = part.astype(jnp.bfloat16)
    copies3 = []
    for i in (4, 3, 5, 2, 6, 1, 7):
        b = lax.rem(z + i, ZS)
        copy = pltpu.make_async_remote_copy(
            src_ref=snd3.at[b], dst_ref=rcv3.at[i - 1],
            send_sem=ss3.at[i - 1], recv_sem=rs3.at[i - 1],
            device_id=far_peer(i), device_id_type=pl.DeviceIdType.MESH,
        )
        copy.start()
        copies3.append(copy)
    result = own3[z]
    for copy in copies3:
        copy.wait()
    for i in range(ZS - 1):
        result = result + rcv3[i].astype(jnp.float32)
    tg_ref[...] = result
    for copy in pg_copies:
        copy.wait()


def fused(text, patches, slots):
    f32, bf16 = jnp.float32, jnp.bfloat16
    vmem = pltpu.VMEM
    dma = pltpu.SemaphoreType.DMA
    return pl.pallas_call(
        kernel,
        out_shape=(
            jax.ShapeDtypeStruct((1, 1), f32),
            jax.ShapeDtypeStruct((2 * CLIP_ROWS, DIM), bf16),
            jax.ShapeDtypeStruct((4, DIM), f32),
        ),
        in_specs=[
            pl.BlockSpec(memory_space=pl.ANY),
            pl.BlockSpec(memory_space=pl.ANY),
            pl.BlockSpec(memory_space=vmem),
        ],
        out_specs=(
            pl.BlockSpec(memory_space=vmem),
            pl.BlockSpec(memory_space=pl.ANY),
            pl.BlockSpec(memory_space=vmem),
        ),
        scratch_shapes=[
            vmem((ROWS, DIM), bf16),
            vmem((4, ROWS, BLOCK), f32),
            vmem((ROWS, DIM), bf16),
            vmem((2 * CLIP_ROWS, DIM), bf16),
            vmem((2, DIM, CLIP_ROWS), bf16),
            vmem((2, FRAMES, BLOCK), f32),
            vmem((ROWS, CAPS), bf16),
            vmem((8, CLIP_ROWS, CHUNK), f32),
            vmem((2, 2, CLIP_ROWS, HALF), bf16),
            vmem((YS, 2, 2, ROWS), f32),
            vmem((XS * CS, 2, CAPS), f32),
            vmem((ZS, 16, CAPS), f32),
            vmem((2, DIM, HALF), f32),
            vmem((2, DIM, HALF), bf16),
            vmem((2, DIM, HALF), bf16),
            vmem((2, 4, HALF), f32),
            vmem((3, DIM, BLOCK), bf16),
            vmem((DIM, BLOCK), f32),
            vmem((3, DIM, BLOCK), bf16),
            vmem((3, 32, DIM), bf16),
            vmem((BLOCK, DIM), f32),
            vmem((3, 32, DIM), bf16),
            vmem((4, 32, BLOCK), f32),
            vmem((ZS, 4, DIM), bf16),
            vmem((ZS, 4, DIM), f32),
            vmem((ZS - 1, 4, DIM), bf16),
            vmem((2 * CLIP_ROWS, DIM), bf16),
            vmem((CLIP_ROWS, ROWS), bf16),
            dma, dma((2,)), dma((2,)),
            dma((3,)), dma((3,)), dma((7,)), dma((7,)), dma((7,)), dma((7,)), dma((2,)), dma((2,)),
            dma((3,)), dma((3,)), dma((3,)), dma((3,)), dma((7,)), dma((7,)),
        ],
        compiler_params=pltpu.CompilerParams(
            collective_id=0, has_side_effects=True, vmem_limit_bytes=52 * 1024 * 1024
        ),
    )(text, patches, slots)


def per_device(text, patches, frame_slots):
    flat = patches.transpose(0, 2, 1, 3).reshape(2 * CLIP_ROWS, DIM)
    loss, grad, text_grad = fused(text, flat, frame_slots)
    grad = grad.reshape(2, PATCH, FRAMES, DIM).transpose(0, 2, 1, 3)
    return loss.reshape(()), grad, text_grad


def solution(mesh):
    finer = Mesh(mesh.devices.reshape(XS, ZS, CS, YS), ("x", "z", "core", "y"))
    clip = ("x", "z", "core")
    in_specs = (P(), P(clip, None, "y", None), P(clip, None))
    out_specs = (P(), P(clip, None, "y", None), P((*clip, "y"), None))
    return jax.shard_map(
        per_device, mesh=finer, in_specs=in_specs, out_specs=out_specs, check_vma=False
    )
```

```python
import jax
import jax.numpy as jnp
from jax import lax
from jax.experimental import pallas as pl
from jax.experimental.pallas import tpu as pltpu
from jax.sharding import Mesh
from jax.sharding import PartitionSpec as P

XS, ZS, CS, YS = 4, 8, 2, 4
WORDS = 8
ROWS = 1024
DIM = 512
FRAMES = 16
PATCH = 49
CLIP_ROWS = FRAMES * PATCH
CAPS = 128
CHUNK = 256
HALF = 512
BLOCK = 128
SCALE = DIM**-0.5
LOG2E = 1.4426950408889634
LN2 = 0.6931471805599453
BIG = 1e30
LOGIT_SCALE = 32.0
LOSS_SCALE = 8192.0
PLANE = sorted(
    ((dx, dy) for dx in range(XS) for dy in range(YS) if dx or dy),
    key=lambda d: (-min(d[0], XS - d[0]) - min(d[1], YS - d[1]), d),
)
NT = (((1,), (1,)), ((), ()))
NN = (((1,), (0,)), ((), ()))
TN = (((0,), (0,)), ((), ()))


def mm(a, b, dims):
    return lax.dot_general(a, b, dims, preferred_element_type=jnp.float32)


def three_parts(value):
    first = value.astype(jnp.bfloat16)
    rest = value - first.astype(jnp.float32)
    second = rest.astype(jnp.bfloat16)
    third = (rest - second.astype(jnp.float32)).astype(jnp.bfloat16)
    return jnp.concatenate([first, second, third], axis=0)


def added_parts(value, rows):
    return value[:rows] + value[rows : 2 * rows] + value[2 * rows : 3 * rows]


def kernel(
    text_hbm, patch_hbm, slots_hbm,
    loss_ref, pg_ref, tg_ref,
    text_in, text_wide, text_perm, patch, slots_ref, bias_ref, member,
    z_ref, gh_ref, cap_rx, near_rx, far_rx,
    t_own, t_send, t_recv, coef_ref, wide_coef,
    snd1, rcv1, sum1, snd2, own2, rcv2, gs_ref,
    text_sem, patch_sem, slots_sem,
    cap_ss, cap_rs, near_ss, near_rs, far_ss, far_rs, core_ss, core_rs,
    ss1, rs1, ss2, rs2,
):
    x = lax.axis_index("x")
    z = lax.axis_index("z")
    core = lax.axis_index("core")
    y = lax.axis_index("y")
    xc = x * CS + core

    text_copy = pltpu.make_async_copy(text_hbm, text_in, text_sem)
    text_copy.start()
    patch_copies = []
    for v in range(2):
        rows = pl.ds(v * CLIP_ROWS, CLIP_ROWS)
        copy = pltpu.make_async_copy(patch_hbm.at[rows], patch.at[rows], patch_sem.at[v])
        copy.start()
        patch_copies.append(copy)
    slots_copy = pltpu.make_async_copy(slots_hbm, slots_ref, slots_sem)
    slots_copy.start()

    def near_peer(i):
        other = lax.rem(xc + i, XS * CS)
        return (other // CS, z, lax.rem(other, CS), y)

    def far_peer(i):
        return (x, lax.rem(z + i, ZS), core, y)

    def cap_peer(i):
        return (x, z, core, lax.rem(y + i, YS))

    def plane_peer(dx, dy):
        return (lax.rem(x + dx, XS), z, core, lax.rem(y + dy, YS))

    barrier = pltpu.get_barrier_semaphore()
    peers = [near_peer(i) for i in range(1, XS * CS)]
    peers += [far_peer(i) for i in range(1, ZS)]
    peers += [plane_peer(dx, dy) for dx in range(XS) for dy in range(1, YS)]
    for peer in peers:
        pl.semaphore_signal(barrier, inc=1, device_id=peer, device_id_type=pl.DeviceIdType.MESH)

    slots_copy.wait()
    slots = slots_ref[...]
    at_row = lax.broadcasted_iota(jnp.int32, (FRAMES, FRAMES), 0)
    at_col = lax.broadcasted_iota(jnp.int32, (FRAMES, FRAMES), 1)
    for v in range(2):
        usable = jnp.where(slots[v : v + 1] >= 0, 0.0, -BIG)
        spread = jnp.where(at_row == at_col, jnp.broadcast_to(usable, (FRAMES, FRAMES)), 0.0)
        column = jnp.sum(spread, axis=1, keepdims=True)
        bias_ref[v] = jnp.broadcast_to(column, (FRAMES, BLOCK))

    q = lax.broadcasted_iota(jnp.int32, (ROWS, CAPS), 0)
    c = lax.broadcasted_iota(jnp.int32, (ROWS, CAPS), 1)
    qh, qx, qy, qz = q // 512, (q // 128) % 4, (q // 32) % 4, q % 8
    caption = qx * 32 + qz * 4 + qh * 2 + qy // 2
    member[...] = jnp.where(caption == c, 1.0, 0.0).astype(jnp.bfloat16)

    text_copy.wait()
    for j in range(4):
        text_wide[j] = text_in[:, j * BLOCK : (j + 1) * BLOCK].astype(jnp.float32)
    for h in range(2):
        for gx in range(4):
            for gy in range(4):
                base = h * 512 + gx * 128 + gy * 32
                for j in range(4):
                    pieces = []
                    for k in range(4):
                        start = gx * 256 + h * 16 + gy * 4 + k
                        pieces.append(text_wide[j, pl.ds(start, 8, stride=32), :])
                    group = jnp.concatenate(pieces, axis=0).astype(jnp.bfloat16)
                    text_perm[base : base + 32, j * BLOCK : (j + 1) * BLOCK] = group

    def tiled(value):
        return jnp.broadcast_to(value, (FRAMES, CHUNK))

    def wide_bias(v):
        part = bias_ref[v]
        return jnp.concatenate([part, part], axis=1)

    def multiply(i):
        v, n = i // 4, i % 4
        z_ref[i] = mm(
            patch[v * CLIP_ROWS : (v + 1) * CLIP_ROWS, :],
            text_perm[n * CHUNK : (n + 1) * CHUNK, :],
            NT,
        )

    def statistics(i):
        v, n = i // 4, i % 4
        top = z_ref[i, 0:FRAMES, :]
        for p in range(1, PATCH):
            top = jnp.maximum(top, z_ref[i, p * FRAMES : (p + 1) * FRAMES, :])
        bias = wide_bias(v)
        peak = jnp.max(top + bias, axis=0, keepdims=True) * (SCALE * LOG2E)
        offset = bias - tiled(peak)
        total = jnp.zeros((FRAMES, CHUNK), jnp.float32)
        weighted = jnp.zeros((FRAMES, CHUNK), jnp.float32)
        for p in range(PATCH):
            s = z_ref[i, p * FRAMES : (p + 1) * FRAMES, :]
            e = jnp.exp2(s * (SCALE * LOG2E) + offset)
            total = total + e
            weighted = weighted + e * s
        total = jnp.sum(total, axis=0, keepdims=True)
        weighted = jnp.sum(weighted, axis=0, keepdims=True)
        lanes = slice(n * CHUNK, (n + 1) * CHUNK)
        cap_rx[y, v, 0:1, lanes] = peak + jnp.log(total) * LOG2E
        cap_rx[y, v, 1:2, lanes] = weighted * SCALE / total

    patch_copies[0].wait()
    multiply(0)
    for i in range(8):
        if i == 3:
            patch_copies[1].wait()
        if i < 7:
            multiply(i + 1)
        statistics(i)

    pl.semaphore_wait(barrier, len(peers))

    cap_copies = []
    for i in range(1, YS):
        copy = pltpu.make_async_remote_copy(
            src_ref=cap_rx.at[y], dst_ref=cap_rx.at[y],
            send_sem=cap_ss.at[i - 1], recv_sem=cap_rs.at[i - 1],
            device_id=cap_peer(i), device_id_type=pl.DeviceIdType.MESH,
        )
        copy.start()
        cap_copies.append(copy)

    for copy in cap_copies:
        copy.wait()

    lse, pooled = [], []
    for v in range(2):
        parts = [cap_rx[j, v, 0:1, :] for j in range(YS)]
        top = jnp.maximum(jnp.maximum(parts[0], parts[1]), jnp.maximum(parts[2], parts[3]))
        factors = [jnp.exp2(part - top) for part in parts]
        total = factors[0] + factors[1] + factors[2] + factors[3]
        mean = factors[0] * cap_rx[0, v, 1:2, :]
        for j in range(1, YS):
            mean = mean + factors[j] * cap_rx[j, v, 1:2, :]
        pooled.append(mean / total)
        lse.append(top + jnp.log(total) * LOG2E)
    both = jnp.concatenate(pooled, axis=0)
    logits_own = added_parts(mm(three_parts(both), member[...], NN), 2) * (LOGIT_SCALE / WORDS)
    near_rx[xc] = logits_own
    near_copies = []
    for i in range(1, XS * CS):
        copy = pltpu.make_async_remote_copy(
            src_ref=near_rx.at[xc], dst_ref=near_rx.at[xc],
            send_sem=near_ss.at[i - 1], recv_sem=near_rs.at[i - 1],
            device_id=near_peer(i), device_id_type=pl.DeviceIdType.MESH,
        )
        copy.start()
        near_copies.append(copy)

    for v in range(2):
        cap_rx[y, v, 0:1, :] = lse[v]
        cap_rx[y, v, 1:2, :] = 1.0 - pooled[v]

    def shaped(half):
        def body(i, _):
            v, m = i // 2, i % 2
            n = half * 2 + m
            lanes = pl.ds(pl.multiple_of(n * CHUNK, CHUNK), CHUNK)
            offset = wide_bias(v) - tiled(cap_rx[y, v, 0:1, lanes])
            shift = tiled(cap_rx[y, v, 1:2, lanes])
            inner = pl.ds(pl.multiple_of(m * CHUNK, CHUNK), CHUNK)
            j = v * 4 + n
            for p in range(PATCH):
                s = z_ref[j, p * FRAMES : (p + 1) * FRAMES, :]
                w = jnp.exp2(s * (SCALE * LOG2E) + offset)
                g = w * (s * SCALE + shift)
                gh_ref[v, half, p * FRAMES : (p + 1) * FRAMES, inner] = g.astype(jnp.bfloat16)
            return 0

        lax.fori_loop(0, 4, body, 0)

    other = 1 - core
    shaped(other)
    core_copies = []
    for v in range(2):
        clip_patch = patch[v * CLIP_ROWS : (v + 1) * CLIP_ROWS, :]
        t_send[v] = mm(gh_ref[v, other], clip_patch, TN).astype(jnp.bfloat16)
        copy = pltpu.make_async_remote_copy(
            src_ref=t_send.at[v], dst_ref=t_recv.at[v],
            send_sem=core_ss.at[v], recv_sem=core_rs.at[v],
            device_id=(x, z, other, y), device_id_type=pl.DeviceIdType.MESH,
        )
        copy.start()
        core_copies.append(copy)

    for copy in near_copies:
        copy.wait()
    far_rx[z] = jnp.concatenate([near_rx[j] for j in range(XS * CS)], axis=0)
    far_copies = []
    for i in range(1, ZS):
        copy = pltpu.make_async_remote_copy(
            src_ref=far_rx.at[z], dst_ref=far_rx.at[z],
            send_sem=far_ss.at[i - 1], recv_sem=far_rs.at[i - 1],
            device_id=far_peer(i), device_id_type=pl.DeviceIdType.MESH,
        )
        copy.start()
        far_copies.append(copy)

    shaped(core)
    for v in range(2):
        t_own[v] = mm(gh_ref[v, core], patch[v * CLIP_ROWS : (v + 1) * CLIP_ROWS, :], TN)

    for copy in far_copies:
        copy.wait()

    logits = jnp.concatenate([far_rx[j] for j in range(ZS)], axis=0)
    row = lax.broadcasted_iota(jnp.int32, (CAPS, CAPS), 0)
    col = lax.broadcasted_iota(jnp.int32, (CAPS, CAPS), 1)
    clip = ((row // 4) % 4) * 32 + (row // 16) * 4 + row % 4
    matched = jnp.sum(jnp.where(clip == col, logits, 0.0), axis=1, keepdims=True)
    cap_top = jnp.max(logits, axis=0, keepdims=True)
    cap_lse = cap_top + jnp.log(jnp.sum(jnp.exp(logits - cap_top), axis=0, keepdims=True))
    clip_top = jnp.max(logits, axis=1, keepdims=True)
    clip_lse = clip_top + jnp.log(jnp.sum(jnp.exp(logits - clip_top), axis=1, keepdims=True))
    terms = jnp.sum(cap_lse, axis=1, keepdims=True) + jnp.sum(clip_lse - 2.0 * matched, axis=0, keepdims=True)
    loss_ref[...] = terms * (0.5 / CAPS)

    near = jnp.concatenate([near_rx[xc], near_rx[x * CS + other]], axis=0)
    near_top = jnp.max(near, axis=1, keepdims=True)
    near_exp = jnp.exp(near - near_top)
    by_clip = near_exp / jnp.sum(near_exp, axis=1, keepdims=True)
    by_cap = jnp.exp(near - cap_lse)
    row = lax.broadcasted_iota(jnp.int32, (4, CAPS), 0)
    col = lax.broadcasted_iota(jnp.int32, (4, CAPS), 1)
    which = jnp.where(row < 2, core, other)
    mine = (x * ZS + z) * 4 + which * 2 + row % 2
    eye = jnp.where(mine == col, 1.0, 0.0)
    grad = (by_clip + by_cap - 2.0 * eye) * (LOSS_SCALE * 0.5 / CAPS * LOGIT_SCALE / WORDS * SCALE)
    parts = three_parts(grad)
    spread = jnp.concatenate(
        [
            jnp.concatenate(
                [jnp.broadcast_to(parts[4 * t + j : 4 * t + j + 1], (BLOCK, CAPS)) for j in range(4)], axis=0
            )
            for t in range(3)
        ],
        axis=1,
    )
    of_half = member[pl.ds(pl.multiple_of(core * HALF, HALF), HALF), :]
    wide_coef[...] = mm(jnp.concatenate([of_half, of_half, of_half], axis=1), spread, NT)

    for copy in core_copies:
        copy.wait()

    def combined(dx, dy):
        block = lax.rem(x + dx, XS) * YS + lax.rem(y + dy, YS)
        rows = pl.ds(pl.multiple_of(block * 32, 32), 32)
        part = jnp.zeros((32, DIM), jnp.float32)
        for j in range(4):
            factor = wide_coef[rows, j * BLOCK : (j + 1) * BLOCK]
            factor = jnp.concatenate([factor] * 4, axis=1)
            source = t_own[j, rows, :] if j < 2 else t_recv[j - 2, rows, :].astype(jnp.float32)
            part = part + factor * source
        return part

    copies1 = []
    for slot, (dx, dy) in enumerate(PLANE):
        snd1[slot] = combined(dx, dy).astype(jnp.bfloat16)
        copy = pltpu.make_async_remote_copy(
            src_ref=snd1.at[slot], dst_ref=rcv1.at[slot],
            send_sem=ss1.at[slot], recv_sem=rs1.at[slot],
            device_id=plane_peer(dx, dy), device_id_type=pl.DeviceIdType.MESH,
        )
        copy.start()
        copies1.append(copy)
    sum1[...] = combined(0, 0)

    coef = added_parts(mm(parts, member[...], NT), 4)
    coef_ref[0] = coef[:, :HALF]
    coef_ref[1] = coef[:, HALF:]
    for v in range(2):
        def scaled(p, _, v=v):
            rows = pl.ds(pl.multiple_of(p * 112, 16), 112)
            for h in range(2):
                g = gh_ref[v, h, rows, :].astype(jnp.float32) * coef_ref[h, v : v + 1, :]
                gs_ref[rows, h * HALF : (h + 1) * HALF] = g.astype(jnp.bfloat16)
            return 0

        lax.fori_loop(0, 7, scaled, 0)
        rows = pl.ds(v * CLIP_ROWS, CLIP_ROWS)
        pg_ref[rows, :] = mm(gs_ref[...], text_perm[...], NN).astype(jnp.bfloat16)

    for copy in copies1:
        copy.wait()
    summed = sum1[...]
    for slot in range(len(PLANE)):
        summed = summed + rcv1[slot].astype(jnp.float32)
    for m in range(4):
        own2[m] = summed[:, m * BLOCK : (m + 1) * BLOCK]
    for j in range(ZS):
        part = jnp.concatenate([own2[m, pl.ds(j, 4, stride=8), :] for m in range(4)], axis=1)
        snd2[j] = part
    copies2 = []
    for i in (4, 3, 5, 2, 6, 1, 7):
        b = lax.rem(z + i, ZS)
        copy = pltpu.make_async_remote_copy(
            src_ref=snd2.at[b], dst_ref=rcv2.at[i - 1],
            send_sem=ss2.at[i - 1], recv_sem=rs2.at[i - 1],
            device_id=far_peer(i), device_id_type=pl.DeviceIdType.MESH,
        )
        copy.start()
        copies2.append(copy)
    result = snd2[z]
    for copy in copies2:
        copy.wait()
    for i in range(ZS - 1):
        result = result + rcv2[i]
    tg_ref[...] = result


def store(loss_in, pg_in, tg_in, loss_out, pg_out, tg_out, sems):
    copies = [
        pltpu.make_async_copy(pg_in, pg_out, sems.at[0]),
        pltpu.make_async_copy(tg_in, tg_out, sems.at[1]),
        pltpu.make_async_copy(loss_in, loss_out, sems.at[2]),
    ]
    for copy in copies:
        copy.start()
    for copy in copies:
        copy.wait()


def fused(text, patches, slots):
    f32, bf16 = jnp.float32, jnp.bfloat16
    vmem = pltpu.VMEM
    dma = pltpu.SemaphoreType.DMA
    shapes = (
        jax.ShapeDtypeStruct((1, 1), f32),
        jax.ShapeDtypeStruct((2 * CLIP_ROWS, DIM), bf16),
        jax.ShapeDtypeStruct((4, DIM), f32),
    )
    results = pl.pallas_call(
        kernel,
        out_shape=shapes,
        in_specs=[pl.BlockSpec(memory_space=pltpu.HBM)] * 3,
        out_specs=(pl.BlockSpec(memory_space=vmem),) * 3,
        scratch_shapes=[
            vmem((ROWS, DIM), bf16),
            vmem((4, ROWS, BLOCK), f32),
            vmem((ROWS, DIM), bf16),
            vmem((2 * CLIP_ROWS, DIM), bf16),
            vmem((2, FRAMES), jnp.int32),
            vmem((2, FRAMES, BLOCK), f32),
            vmem((ROWS, CAPS), bf16),
            vmem((8, CLIP_ROWS, CHUNK), f32),
            vmem((2, 2, CLIP_ROWS, HALF), bf16),
            vmem((YS, 2, 2, ROWS), f32),
            vmem((XS * CS, 2, CAPS), f32),
            vmem((ZS, 16, CAPS), f32),
            vmem((2, HALF, DIM), f32),
            vmem((2, HALF, DIM), bf16),
            vmem((2, HALF, DIM), bf16),
            vmem((2, 4, HALF), f32),
            vmem((HALF, 4 * BLOCK), f32),
            vmem((15, 32, DIM), bf16),
            vmem((15, 32, DIM), bf16),
            vmem((32, DIM), f32),
            vmem((ZS, 4, DIM), f32),
            vmem((4, 32, BLOCK), f32),
            vmem((ZS - 1, 4, DIM), f32),
            vmem((CLIP_ROWS, ROWS), bf16),
            dma, dma((2,)), dma,
            dma((3,)), dma((3,)), dma((7,)), dma((7,)), dma((7,)), dma((7,)), dma((2,)), dma((2,)),
            dma((15,)), dma((15,)), dma((7,)), dma((7,)),
        ],
        compiler_params=pltpu.CompilerParams(
            collective_id=0, has_side_effects=True, vmem_limit_bytes=44 * 1024 * 1024
        ),
    )(*[pltpu.with_memory_space_constraint(a, pltpu.HBM) for a in (text, patches, slots)])
    return pl.pallas_call(
        store,
        out_shape=shapes,
        in_specs=[pl.BlockSpec(memory_space=pl.ANY)] * 3,
        out_specs=(pl.BlockSpec(memory_space=pl.ANY),) * 3,
        scratch_shapes=[dma((3,))],
    )(*[pltpu.with_memory_space_constraint(a, pltpu.VMEM) for a in results])


def per_device(text, patches, frame_slots):
    flat = patches.transpose(0, 2, 1, 3).reshape(2 * CLIP_ROWS, DIM)
    loss, grad, text_grad = fused(text, flat, frame_slots)
    grad = grad.reshape(2, PATCH, FRAMES, DIM).transpose(0, 2, 1, 3)
    return loss.reshape(()), grad, text_grad


def solution(mesh):
    finer = Mesh(mesh.devices.reshape(XS, ZS, CS, YS), ("x", "z", "core", "y"))
    clip = ("x", "z", "core")
    in_specs = (P(), P(clip, None, "y", None), P(clip, None))
    out_specs = (P(), P(clip, None, "y", None), P((*clip, "y"), None))
    return jax.shard_map(
        per_device, mesh=finer, in_specs=in_specs, out_specs=out_specs, check_vma=False
    )
```

```python
import jax
import jax.numpy as jnp
from jax import lax
from jax.experimental import pallas as pl
from jax.experimental.pallas import tpu as pltpu
from jax.sharding import Mesh
from jax.sharding import PartitionSpec as P

XS, ZS, CS, YS = 4, 8, 2, 4
WORDS = 8
ROWS = 1024
DIM = 512
FRAMES = 16
PATCH = 49
CLIP_ROWS = FRAMES * PATCH
CAPS = 128
CHUNK = 256
HALF = 512
BLOCK = 128
SCALE = DIM**-0.5
LOG2E = 1.4426950408889634
LN2 = 0.6931471805599453
BIG = 1e30
LOGIT_SCALE = 32.0
LOSS_SCALE = 8192.0
CHIP_COUNT = XS * ZS
CHIPS = sorted(
    ((dx, dz) for dx in range(XS) for dz in range(ZS) if dx or dz),
    key=lambda d: (-min(d[0], XS - d[0]) - min(d[1], ZS - d[1]), d),
)
PLANE = sorted(
    ((dx, dy) for dx in range(XS) for dy in range(YS) if dx or dy),
    key=lambda d: (-min(d[0], XS - d[0]) - min(d[1], YS - d[1]), d),
)
NT = (((1,), (1,)), ((), ()))
NN = (((1,), (0,)), ((), ()))
TN = (((0,), (0,)), ((), ()))


def mm(a, b, dims):
    return lax.dot_general(a, b, dims, preferred_element_type=jnp.float32)


def three_parts(value):
    first = value.astype(jnp.bfloat16)
    rest = value - first.astype(jnp.float32)
    second = rest.astype(jnp.bfloat16)
    third = (rest - second.astype(jnp.float32)).astype(jnp.bfloat16)
    return jnp.concatenate([first, second, third], axis=0)


def added_parts(value, rows):
    return value[:rows] + value[rows : 2 * rows] + value[2 * rows : 3 * rows]


def kernel(
    text_hbm, patch_hbm, slots_hbm,
    loss_ref, pg_ref, tg_ref,
    text_in, text_wide, text_perm, patch, slots_ref, bias_ref, member,
    z_ref, gh_ref, cap_rx, pair_rx, chip_rx,
    t_own, t_send, t_recv, coef_ref, wide_coef,
    snd1, rcv1, sum1, snd2, own2, own3, rcv2, gs_ref,
    text_sem, patch_sem, slots_sem,
    cap_ss, cap_rs, pair_ss, pair_rs, chip_ss, chip_rs, core_ss, core_rs,
    ss1, rs1, ss2, rs2,
):
    x = lax.axis_index("x")
    z = lax.axis_index("z")
    core = lax.axis_index("core")
    y = lax.axis_index("y")
    other = 1 - core
    chip = x * ZS + z

    slots_copy = pltpu.make_async_copy(slots_hbm, slots_ref, slots_sem)
    text_copies, patch_copies = [], []

    def fetch_text(n):
        rows = pl.ds(n * CHUNK, CHUNK)
        text_copies.append(pltpu.make_async_copy(text_hbm.at[rows], text_in.at[rows], text_sem.at[n]))
        text_copies[-1].start()

    def fetch_patch(v):
        rows = pl.ds(v * CLIP_ROWS, CLIP_ROWS)
        patch_copies.append(pltpu.make_async_copy(patch_hbm.at[rows], patch.at[rows], patch_sem.at[v]))
        patch_copies[-1].start()

    fetch_text(0)
    slots_copy.start()
    fetch_patch(0)
    for n in range(1, XS):
        fetch_text(n)
    fetch_patch(1)

    def far_peer(i):
        return (x, lax.rem(z + i, ZS), core, y)

    def cap_peer(i):
        return (x, z, core, lax.rem(y + i, YS))

    def plane_peer(dx, dy):
        return (lax.rem(x + dx, XS), z, core, lax.rem(y + dy, YS))

    def chip_peer(dx, dz):
        return (lax.rem(x + dx, XS), lax.rem(z + dz, ZS), core, y)

    twin = (x, z, other, y)

    barrier = pltpu.get_barrier_semaphore()
    peers = [chip_peer(dx, dz) for dx, dz in CHIPS]
    peers += [plane_peer(dx, dy) for dx, dy in PLANE if dy]
    peers.append(twin)
    for peer in peers:
        pl.semaphore_signal(barrier, inc=1, device_id=peer, device_id_type=pl.DeviceIdType.MESH)

    def arrange(gx):
        text_copies[gx].wait()
        rows = slice(gx * CHUNK, (gx + 1) * CHUNK)
        for j in range(4):
            text_wide[j, rows, :] = text_in[rows, j * BLOCK : (j + 1) * BLOCK].astype(jnp.float32)
        for h in range(2):
            for gy in range(4):
                base = gx * CHUNK + h * BLOCK + gy * 32
                for j in range(4):
                    pieces = []
                    for k in range(4):
                        start = gx * CHUNK + h * 16 + gy * 4 + k
                        pieces.append(text_wide[j, pl.ds(start, 8, stride=32), :])
                    group = jnp.concatenate(pieces, axis=0).astype(jnp.bfloat16)
                    text_perm[base : base + 32, j * BLOCK : (j + 1) * BLOCK] = group

    def tiled(value):
        return jnp.broadcast_to(value, (FRAMES, CHUNK))

    def wide_bias(v):
        part = bias_ref[v]
        return jnp.concatenate([part, part], axis=1)

    def multiply(i):
        v, n = i // 4, i % 4
        z_ref[i] = mm(
            patch[v * CLIP_ROWS : (v + 1) * CLIP_ROWS, :],
            text_perm[n * CHUNK : (n + 1) * CHUNK, :],
            NT,
        )

    def statistics(i):
        v, n = i // 4, i % 4
        top = z_ref[i, 0:FRAMES, :]
        for p in range(1, PATCH):
            top = jnp.maximum(top, z_ref[i, p * FRAMES : (p + 1) * FRAMES, :])
        bias = wide_bias(v)
        peak = jnp.max(top + bias, axis=0, keepdims=True) * (SCALE * LOG2E)
        offset = bias - tiled(peak)
        total = jnp.zeros((FRAMES, CHUNK), jnp.float32)
        weighted = jnp.zeros((FRAMES, CHUNK), jnp.float32)
        for p in range(PATCH):
            s = z_ref[i, p * FRAMES : (p + 1) * FRAMES, :]
            e = jnp.exp2(s * (SCALE * LOG2E) + offset)
            total = total + e
            weighted = weighted + e * s
        total = jnp.sum(total, axis=0, keepdims=True)
        weighted = jnp.sum(weighted, axis=0, keepdims=True)
        lanes = slice(n * CHUNK, (n + 1) * CHUNK)
        cap_rx[y, v, 0:1, lanes] = peak + jnp.log(total) * LOG2E
        cap_rx[y, v, 1:2, lanes] = weighted * SCALE / total

    arrange(0)
    slots_copy.wait()
    slots = slots_ref[...]
    at_row = lax.broadcasted_iota(jnp.int32, (FRAMES, FRAMES), 0)
    at_col = lax.broadcasted_iota(jnp.int32, (FRAMES, FRAMES), 1)
    for v in range(2):
        usable = jnp.where(slots[v : v + 1] >= 0, 0.0, -BIG)
        spread = jnp.where(at_row == at_col, jnp.broadcast_to(usable, (FRAMES, FRAMES)), 0.0)
        column = jnp.sum(spread, axis=1, keepdims=True)
        bias_ref[v] = jnp.broadcast_to(column, (FRAMES, BLOCK))

    patch_copies[0].wait()
    multiply(0)
    for i in range(8):
        if i < 3:
            arrange(i + 1)
        if i == 3:
            patch_copies[1].wait()
        if i < 7:
            multiply(i + 1)
        statistics(i)

    pl.semaphore_wait(barrier, len(peers))

    cap_copies = []
    for i in range(1, YS):
        copy = pltpu.make_async_remote_copy(
            src_ref=cap_rx.at[y], dst_ref=cap_rx.at[y],
            send_sem=cap_ss.at[i - 1], recv_sem=cap_rs.at[i - 1],
            device_id=cap_peer(i), device_id_type=pl.DeviceIdType.MESH,
        )
        copy.start()
        cap_copies.append(copy)

    q = lax.broadcasted_iota(jnp.int32, (ROWS, CAPS), 0)
    c = lax.broadcasted_iota(jnp.int32, (ROWS, CAPS), 1)
    qx, qh, qy, qz = q // 256, (q // 128) % 2, (q // 32) % 4, q % 8
    caption = qx * 32 + qz * 4 + qh * 2 + qy // 2
    member[...] = jnp.where(caption == c, 1.0, 0.0).astype(jnp.bfloat16)

    for copy in cap_copies:
        copy.wait()

    lse, pooled = [], []
    for v in range(2):
        parts = [cap_rx[j, v, 0:1, :] for j in range(YS)]
        top = jnp.maximum(jnp.maximum(parts[0], parts[1]), jnp.maximum(parts[2], parts[3]))
        factors = [jnp.exp2(part - top) for part in parts]
        total = factors[0] + factors[1] + factors[2] + factors[3]
        mean = factors[0] * cap_rx[0, v, 1:2, :]
        for j in range(1, YS):
            mean = mean + factors[j] * cap_rx[j, v, 1:2, :]
        pooled.append(mean / total)
        lse.append(top + jnp.log(total) * LOG2E)
    both = jnp.concatenate(pooled, axis=0)
    logits_own = added_parts(mm(three_parts(both), member[...], NN), 2) * (LOGIT_SCALE / WORDS)
    pair_rx[core] = logits_own
    pair_copy = pltpu.make_async_remote_copy(
        src_ref=pair_rx.at[core], dst_ref=pair_rx.at[core],
        send_sem=pair_ss, recv_sem=pair_rs,
        device_id=twin, device_id_type=pl.DeviceIdType.MESH,
    )
    pair_copy.start()

    for v in range(2):
        cap_rx[y, v, 0:1, :] = lse[v]
        cap_rx[y, v, 1:2, :] = 1.0 - pooled[v]

    def shaped(v, half):
        def body(n, _):
            lanes = pl.ds(pl.multiple_of(n * CHUNK + half * BLOCK, BLOCK), BLOCK)
            near = pl.ds(pl.multiple_of(half * BLOCK, BLOCK), BLOCK)
            inner = pl.ds(pl.multiple_of(n * BLOCK, BLOCK), BLOCK)
            offset = bias_ref[v] - jnp.broadcast_to(cap_rx[y, v, 0:1, lanes], (FRAMES, BLOCK))
            shift = jnp.broadcast_to(cap_rx[y, v, 1:2, lanes], (FRAMES, BLOCK))
            for p in range(PATCH):
                s = z_ref[v * 4 + n, p * FRAMES : (p + 1) * FRAMES, near]
                w = jnp.exp2(s * (SCALE * LOG2E) + offset)
                g = w * (s * SCALE + shift)
                gh_ref[v, half, p * FRAMES : (p + 1) * FRAMES, inner] = g.astype(jnp.bfloat16)
            return 0

        lax.fori_loop(0, 4, body, 0)

    shaped(0, other)
    pair_copy.wait()
    chip_rx[chip] = jnp.concatenate([pair_rx[0], pair_rx[1]], axis=0)
    chip_copies = []
    for slot, (dx, dz) in enumerate(CHIPS):
        copy = pltpu.make_async_remote_copy(
            src_ref=chip_rx.at[chip], dst_ref=chip_rx.at[chip],
            send_sem=chip_ss.at[slot], recv_sem=chip_rs.at[slot],
            device_id=chip_peer(dx, dz), device_id_type=pl.DeviceIdType.MESH,
        )
        copy.start()
        chip_copies.append(copy)

    core_copies = []
    for v in range(2):
        if v:
            shaped(v, other)
        clip_patch = patch[v * CLIP_ROWS : (v + 1) * CLIP_ROWS, :]
        t_send[v] = mm(gh_ref[v, other], clip_patch, TN).astype(jnp.bfloat16)
        copy = pltpu.make_async_remote_copy(
            src_ref=t_send.at[v], dst_ref=t_recv.at[v],
            send_sem=core_ss.at[v], recv_sem=core_rs.at[v],
            device_id=twin, device_id_type=pl.DeviceIdType.MESH,
        )
        copy.start()
        core_copies.append(copy)

    for v in range(2):
        shaped(v, core)
        t_own[v] = mm(gh_ref[v, core], patch[v * CLIP_ROWS : (v + 1) * CLIP_ROWS, :], TN)

    for copy in chip_copies:
        copy.wait()

    blocks = [chip_rx[j] for j in range(CHIP_COUNT)]
    cap_top = blocks[0]
    for block in blocks[1:]:
        cap_top = jnp.maximum(cap_top, block)
    cap_top = jnp.max(cap_top, axis=0, keepdims=True)
    cap_sum = jnp.exp(blocks[0] - cap_top)
    for block in blocks[1:]:
        cap_sum = cap_sum + jnp.exp(block - cap_top)
    cap_lse = cap_top + jnp.log(jnp.sum(cap_sum, axis=0, keepdims=True))
    row = lax.broadcasted_iota(jnp.int32, (4, CAPS), 0)
    col = lax.broadcasted_iota(jnp.int32, (4, CAPS), 1)
    near = chip_rx[chip]
    near_top = jnp.max(near, axis=1, keepdims=True)
    near_exp = jnp.exp(near - near_top)
    by_clip = near_exp / jnp.sum(near_exp, axis=1, keepdims=True)
    by_cap = jnp.exp(near - cap_lse)
    eye = jnp.where(chip * 4 + row == col, 1.0, 0.0)
    grad = (by_clip + by_cap - 2.0 * eye) * (LOSS_SCALE * 0.5 / CAPS * LOGIT_SCALE / WORDS * SCALE)
    parts = three_parts(grad)
    spread = jnp.concatenate(
        [
            jnp.concatenate(
                [jnp.broadcast_to(parts[4 * t + j : 4 * t + j + 1], (BLOCK, CAPS)) for j in range(4)], axis=0
            )
            for t in range(3)
        ],
        axis=1,
    )
    of_half = jnp.concatenate(
        [member[pl.ds(pl.multiple_of(gx * CHUNK + core * BLOCK, BLOCK), BLOCK), :] for gx in range(XS)], axis=0
    )
    wide_coef[...] = mm(jnp.concatenate([of_half, of_half, of_half], axis=1), spread, NT)

    for copy in core_copies:
        copy.wait()

    def combined(dx, dy):
        block = lax.rem(x + dx, XS) * YS + lax.rem(y + dy, YS)
        rows = pl.ds(pl.multiple_of(block * 32, 32), 32)
        part = jnp.zeros((32, DIM), jnp.float32)
        for j in range(4):
            which = core * 2 + j if j < 2 else other * 2 + j - 2
            factor = wide_coef[rows, pl.ds(pl.multiple_of(which * BLOCK, BLOCK), BLOCK)]
            factor = jnp.concatenate([factor] * 4, axis=1)
            source = t_own[j, rows, :] if j < 2 else t_recv[j - 2, rows, :].astype(jnp.float32)
            part = part + factor * source
        return part

    copies1 = []
    for slot, (dx, dy) in enumerate(PLANE):
        snd1[slot] = combined(dx, dy).astype(jnp.bfloat16)
        copy = pltpu.make_async_remote_copy(
            src_ref=snd1.at[slot], dst_ref=rcv1.at[slot],
            send_sem=ss1.at[slot], recv_sem=rs1.at[slot],
            device_id=plane_peer(dx, dy), device_id_type=pl.DeviceIdType.MESH,
        )
        copy.start()
        copies1.append(copy)
    sum1[...] = combined(0, 0)

    coef = added_parts(mm(parts, member[...], NT), 4)
    for j in range(4):
        coef_ref[j] = coef[j : j + 1]
    for v in range(2):
        def scaled(p, _, v=v):
            rows = pl.ds(pl.multiple_of(p * 112, 16), 112)
            for gx in range(XS):
                for h in range(2):
                    lanes = slice(gx * CHUNK + h * BLOCK, gx * CHUNK + (h + 1) * BLOCK)
                    g = gh_ref[v, h, rows, gx * BLOCK : (gx + 1) * BLOCK].astype(jnp.float32)
                    gs_ref[rows, lanes] = (g * coef_ref[core * 2 + v, :, lanes]).astype(jnp.bfloat16)
            return 0

        lax.fori_loop(0, 7, scaled, 0)
        rows = pl.ds(v * CLIP_ROWS, CLIP_ROWS)
        pg_ref[rows, :] = mm(gs_ref[...], text_perm[...], NN).astype(jnp.bfloat16)

    terms = jnp.sum(cap_lse, axis=1, keepdims=True)
    for j, block in enumerate(blocks):
        clip_top = jnp.max(block, axis=1, keepdims=True)
        clip_lse = clip_top + jnp.log(jnp.sum(jnp.exp(block - clip_top), axis=1, keepdims=True))
        matched = jnp.sum(jnp.where(row + 4 * j == col, block, 0.0), axis=1, keepdims=True)
        terms = terms + jnp.sum(clip_lse - 2.0 * matched, axis=0, keepdims=True)
    loss_ref[...] = terms * (0.5 / CAPS)

    for copy in copies1:
        copy.wait()
    summed = sum1[...]
    for slot in range(len(PLANE)):
        summed = summed + rcv1[slot].astype(jnp.float32)
    for m in range(4):
        own2[m] = summed[:, m * BLOCK : (m + 1) * BLOCK]
    for j in range(ZS):
        part = jnp.concatenate([own2[m, pl.ds(j, 4, stride=8), :] for m in range(4)], axis=1)
        own3[j] = part
        snd2[j] = part.astype(jnp.bfloat16)
    copies2 = []
    for i in (4, 3, 5, 2, 6, 1, 7):
        b = lax.rem(z + i, ZS)
        copy = pltpu.make_async_remote_copy(
            src_ref=snd2.at[b], dst_ref=rcv2.at[i - 1],
            send_sem=ss2.at[i - 1], recv_sem=rs2.at[i - 1],
            device_id=far_peer(i), device_id_type=pl.DeviceIdType.MESH,
        )
        copy.start()
        copies2.append(copy)
    result = own3[z]
    for copy in copies2:
        copy.wait()
    for i in range(ZS - 1):
        result = result + rcv2[i].astype(jnp.float32)
    tg_ref[...] = result


def store(loss_in, pg_in, tg_in, loss_out, pg_out, tg_out, sems):
    copies = [
        pltpu.make_async_copy(pg_in, pg_out, sems.at[0]),
        pltpu.make_async_copy(tg_in, tg_out, sems.at[1]),
        pltpu.make_async_copy(loss_in, loss_out, sems.at[2]),
    ]
    for copy in copies:
        copy.start()
    for copy in copies:
        copy.wait()


def fused(text, patches, slots):
    f32, bf16 = jnp.float32, jnp.bfloat16
    vmem = pltpu.VMEM
    dma = pltpu.SemaphoreType.DMA
    shapes = (
        jax.ShapeDtypeStruct((1, 1), f32),
        jax.ShapeDtypeStruct((2 * CLIP_ROWS, DIM), bf16),
        jax.ShapeDtypeStruct((4, DIM), f32),
    )
    results = pl.pallas_call(
        kernel,
        out_shape=shapes,
        in_specs=[pl.BlockSpec(memory_space=pltpu.HBM)] * 3,
        out_specs=(pl.BlockSpec(memory_space=vmem),) * 3,
        scratch_shapes=[
            vmem((ROWS, DIM), bf16),
            vmem((4, ROWS, BLOCK), f32),
            vmem((ROWS, DIM), bf16),
            vmem((2 * CLIP_ROWS, DIM), bf16),
            vmem((2, FRAMES), jnp.int32),
            vmem((2, FRAMES, BLOCK), f32),
            vmem((ROWS, CAPS), bf16),
            vmem((8, CLIP_ROWS, CHUNK), f32),
            vmem((2, 2, CLIP_ROWS, HALF), bf16),
            vmem((YS, 2, 2, ROWS), f32),
            vmem((CS, 2, CAPS), f32),
            vmem((CHIP_COUNT, 4, CAPS), f32),
            vmem((2, HALF, DIM), f32),
            vmem((2, HALF, DIM), bf16),
            vmem((2, HALF, DIM), bf16),
            vmem((4, 1, ROWS), f32),
            vmem((HALF, 4 * BLOCK), f32),
            vmem((15, 32, DIM), bf16),
            vmem((15, 32, DIM), bf16),
            vmem((32, DIM), f32),
            vmem((ZS, 4, DIM), bf16),
            vmem((4, 32, BLOCK), f32),
            vmem((ZS, 4, DIM), f32),
            vmem((ZS - 1, 4, DIM), bf16),
            vmem((CLIP_ROWS, ROWS), bf16),
            dma((4,)), dma((2,)), dma,
            dma((3,)), dma((3,)), dma, dma, dma((31,)), dma((31,)), dma((2,)), dma((2,)),
            dma((15,)), dma((15,)), dma((7,)), dma((7,)),
        ],
        compiler_params=pltpu.CompilerParams(
            collective_id=0, has_side_effects=True, vmem_limit_bytes=44 * 1024 * 1024
        ),
    )(*[pltpu.with_memory_space_constraint(a, pltpu.HBM) for a in (text, patches, slots)])
    return pl.pallas_call(
        store,
        out_shape=shapes,
        in_specs=[pl.BlockSpec(memory_space=pl.ANY)] * 3,
        out_specs=(pl.BlockSpec(memory_space=pl.ANY),) * 3,
        scratch_shapes=[dma((3,))],
    )(*[pltpu.with_memory_space_constraint(a, pltpu.VMEM) for a in results])


def per_device(text, patches, frame_slots):
    flat = patches.transpose(0, 2, 1, 3).reshape(2 * CLIP_ROWS, DIM)
    loss, grad, text_grad = fused(text, flat, frame_slots)
    grad = grad.reshape(2, PATCH, FRAMES, DIM).transpose(0, 2, 1, 3)
    return loss.reshape(()), grad, text_grad


def solution(mesh):
    finer = Mesh(mesh.devices.reshape(XS, ZS, CS, YS), ("x", "z", "core", "y"))
    clip = ("x", "z", "core")
    in_specs = (P(), P(clip, None, "y", None), P(clip, None))
    out_specs = (P(), P(clip, None, "y", None), P((*clip, "y"), None))
    return jax.shard_map(
        per_device, mesh=finer, in_specs=in_specs, out_specs=out_specs, check_vma=False
    )
```

```python
import jax
import jax.numpy as jnp
from jax import lax
from jax.experimental import pallas as pl
from jax.experimental.pallas import tpu as pltpu
from jax.sharding import Mesh
from jax.sharding import PartitionSpec as P

XS, ZS, CS, YS = 4, 8, 2, 4
WORDS = 8
ROWS = 1024
DIM = 512
FRAMES = 16
PATCH = 49
CLIP_ROWS = FRAMES * PATCH
CAPS = 128
CHUNK = 256
HALF = 512
BLOCK = 128
SCALE = DIM**-0.5
LOG2E = 1.4426950408889634
LN2 = 0.6931471805599453
BIG = 1e30
LOGIT_SCALE = 32.0
LOSS_SCALE = 8192.0
CHIP_COUNT = XS * ZS
CHIPS = sorted(
    ((dx, dz) for dx in range(XS) for dz in range(ZS) if dx or dz),
    key=lambda d: (-min(d[0], XS - d[0]) - min(d[1], ZS - d[1]), d),
)
PLANE = sorted(
    ((dx, dy) for dx in range(XS) for dy in range(YS) if dx or dy),
    key=lambda d: (-min(d[0], XS - d[0]) - min(d[1], YS - d[1]), d),
)
NT = (((1,), (1,)), ((), ()))
NN = (((1,), (0,)), ((), ()))
TN = (((0,), (0,)), ((), ()))


def mm(a, b, dims):
    return lax.dot_general(a, b, dims, preferred_element_type=jnp.float32)


def three_parts(value):
    first = value.astype(jnp.bfloat16)
    rest = value - first.astype(jnp.float32)
    second = rest.astype(jnp.bfloat16)
    third = (rest - second.astype(jnp.float32)).astype(jnp.bfloat16)
    return jnp.concatenate([first, second, third], axis=0)


def added_parts(value, rows):
    return value[:rows] + value[rows : 2 * rows] + value[2 * rows : 3 * rows]


def kernel(
    text_hbm, patch_hbm, slots_hbm,
    loss_ref, pg_ref, tg_ref,
    text_in, text_perm, patch, slots_ref, bias_ref, member,
    z_ref, gh_ref, cap_rx, pair_rx, chip_rx, local,
    t_own, t_send, t_recv, coef_ref, wide_coef,
    snd1, rcv1, sum1, snd2, own2, own3, rcv2, gs_ref,
    text_sem, patch_sem, slots_sem,
    cap_ss, cap_rs, pair_ss, pair_rs, chip_ss, chip_rs, core_ss, core_rs,
    ss1, rs1, ss2, rs2,
):
    x = lax.axis_index("x")
    z = lax.axis_index("z")
    core = lax.axis_index("core")
    y = lax.axis_index("y")
    other = 1 - core
    chip = x * ZS + z

    slots_copy = pltpu.make_async_copy(slots_hbm, slots_ref, slots_sem)
    text_copies, patch_copies = [], []

    def fetch_text(n):
        rows = pl.ds(n * CHUNK, CHUNK)
        text_copies.append(pltpu.make_async_copy(text_hbm.at[rows], text_in.at[rows], text_sem.at[n]))
        text_copies[-1].start()

    def fetch_patch(v):
        rows = pl.ds(v * CLIP_ROWS, CLIP_ROWS)
        patch_copies.append(pltpu.make_async_copy(patch_hbm.at[rows], patch.at[rows], patch_sem.at[v]))
        patch_copies[-1].start()

    fetch_text(0)
    slots_copy.start()
    fetch_patch(0)
    for n in range(1, XS):
        fetch_text(n)
    fetch_patch(1)

    def far_peer(i):
        return (x, lax.rem(z + i, ZS), core, y)

    def cap_peer(i):
        return (x, z, core, lax.rem(y + i, YS))

    def plane_peer(dx, dy):
        return (lax.rem(x + dx, XS), z, core, lax.rem(y + dy, YS))

    def chip_peer(dx, dz):
        return (lax.rem(x + dx, XS), lax.rem(z + dz, ZS), core, y)

    twin = (x, z, other, y)

    barrier = pltpu.get_barrier_semaphore()
    peers = [chip_peer(dx, dz) for dx, dz in CHIPS]
    peers += [plane_peer(dx, dy) for dx, dy in PLANE if dy]
    peers.append(twin)
    for peer in peers:
        pl.semaphore_signal(barrier, inc=1, device_id=peer, device_id_type=pl.DeviceIdType.MESH)

    q = lax.broadcasted_iota(jnp.int32, (CHUNK, CHUNK), 0)
    r = lax.broadcasted_iota(jnp.int32, (CHUNK, CHUNK), 1)
    source = (q % 8) * 32 + (q // 32) * 4 + (q // 8) % 4
    order = jnp.where(source == r, 1.0, 0.0).astype(jnp.bfloat16)

    def arrange(gx):
        text_copies[gx].wait()
        rows = slice(gx * CHUNK, (gx + 1) * CHUNK)
        text_perm[rows, :] = mm(order, text_in[rows, :], NN).astype(jnp.bfloat16)

    def tiled(value):
        return jnp.broadcast_to(value, (FRAMES, CHUNK))

    def wide_bias(v):
        part = bias_ref[v]
        return jnp.concatenate([part, part], axis=1)

    def multiply(i):
        v, n = i // 4, i % 4
        z_ref[i] = mm(
            patch[v * CLIP_ROWS : (v + 1) * CLIP_ROWS, :],
            text_perm[n * CHUNK : (n + 1) * CHUNK, :],
            NT,
        )

    def statistics(i):
        v, n = i // 4, i % 4
        top = z_ref[i, 0:FRAMES, :]
        for p in range(1, PATCH):
            top = jnp.maximum(top, z_ref[i, p * FRAMES : (p + 1) * FRAMES, :])
        bias = wide_bias(v)
        peak = jnp.max(top + bias, axis=0, keepdims=True) * (SCALE * LOG2E)
        offset = bias - tiled(peak)
        total = jnp.zeros((FRAMES, CHUNK), jnp.float32)
        weighted = jnp.zeros((FRAMES, CHUNK), jnp.float32)
        for p in range(PATCH):
            s = z_ref[i, p * FRAMES : (p + 1) * FRAMES, :]
            e = jnp.exp2(s * (SCALE * LOG2E) + offset)
            total = total + e
            weighted = weighted + e * s
        total = jnp.sum(total, axis=0, keepdims=True)
        weighted = jnp.sum(weighted, axis=0, keepdims=True)
        lanes = slice(n * CHUNK, (n + 1) * CHUNK)
        local[v, 0:1, lanes] = peak + jnp.log(total) * LOG2E
        local[v, 1:2, lanes] = weighted * SCALE / total

    arrange(0)
    slots_copy.wait()
    slots = slots_ref[...]
    at_row = lax.broadcasted_iota(jnp.int32, (FRAMES, FRAMES), 0)
    at_col = lax.broadcasted_iota(jnp.int32, (FRAMES, FRAMES), 1)
    for v in range(2):
        usable = jnp.where(slots[v : v + 1] >= 0, 0.0, -BIG)
        spread = jnp.where(at_row == at_col, jnp.broadcast_to(usable, (FRAMES, FRAMES)), 0.0)
        column = jnp.sum(spread, axis=1, keepdims=True)
        bias_ref[v] = jnp.broadcast_to(column, (FRAMES, BLOCK))

    for n in range(1, XS):
        arrange(n)
    patch_copies[0].wait()
    patch_copies[1].wait()
    multiply(0)
    for i in range(8):
        if i < 7:
            multiply(i + 1)
        statistics(i)

    cap_rx[y] = local[...]
    pl.semaphore_wait(barrier, len(peers))

    cap_copies = []
    for i in range(1, YS):
        copy = pltpu.make_async_remote_copy(
            src_ref=cap_rx.at[y], dst_ref=cap_rx.at[y],
            send_sem=cap_ss.at[i - 1], recv_sem=cap_rs.at[i - 1],
            device_id=cap_peer(i), device_id_type=pl.DeviceIdType.MESH,
        )
        copy.start()
        cap_copies.append(copy)

    q = lax.broadcasted_iota(jnp.int32, (ROWS, CAPS), 0)
    c = lax.broadcasted_iota(jnp.int32, (ROWS, CAPS), 1)
    qx, qh, qy, qz = q // 256, (q // 128) % 2, (q // 32) % 4, q % 8
    caption = qx * 32 + qz * 4 + qh * 2 + qy // 2
    member[...] = jnp.where(caption == c, 1.0, 0.0).astype(jnp.bfloat16)

    for copy in cap_copies:
        copy.wait()

    lse, pooled = [], []
    for v in range(2):
        parts = [cap_rx[j, v, 0:1, :] for j in range(YS)]
        top = jnp.maximum(jnp.maximum(parts[0], parts[1]), jnp.maximum(parts[2], parts[3]))
        factors = [jnp.exp2(part - top) for part in parts]
        total = factors[0] + factors[1] + factors[2] + factors[3]
        mean = factors[0] * cap_rx[0, v, 1:2, :]
        for j in range(1, YS):
            mean = mean + factors[j] * cap_rx[j, v, 1:2, :]
        pooled.append(mean / total)
        lse.append(top + jnp.log(total) * LOG2E)
    both = jnp.concatenate(pooled, axis=0)
    logits_own = added_parts(mm(three_parts(both), member[...], NN), 2) * (LOGIT_SCALE / WORDS)
    pair_rx[core] = logits_own
    pair_copy = pltpu.make_async_remote_copy(
        src_ref=pair_rx.at[core], dst_ref=pair_rx.at[core],
        send_sem=pair_ss, recv_sem=pair_rs,
        device_id=twin, device_id_type=pl.DeviceIdType.MESH,
    )
    pair_copy.start()

    for v in range(2):
        cap_rx[y, v, 0:1, :] = lse[v]
        cap_rx[y, v, 1:2, :] = 1.0 - pooled[v]

    def shaped(v, half):
        def body(n, _):
            lanes = pl.ds(pl.multiple_of(n * CHUNK + half * BLOCK, BLOCK), BLOCK)
            near = pl.ds(pl.multiple_of(half * BLOCK, BLOCK), BLOCK)
            inner = pl.ds(pl.multiple_of(n * BLOCK, BLOCK), BLOCK)
            offset = bias_ref[v] - jnp.broadcast_to(cap_rx[y, v, 0:1, lanes], (FRAMES, BLOCK))
            shift = jnp.broadcast_to(cap_rx[y, v, 1:2, lanes], (FRAMES, BLOCK))
            for p in range(PATCH):
                s = z_ref[v * 4 + n, p * FRAMES : (p + 1) * FRAMES, near]
                w = jnp.exp2(s * (SCALE * LOG2E) + offset)
                g = w * (s * SCALE + shift)
                gh_ref[v, half, p * FRAMES : (p + 1) * FRAMES, inner] = g.astype(jnp.bfloat16)
            return 0

        lax.fori_loop(0, 4, body, 0)

    pair_copy.wait()
    chip_rx[chip] = jnp.concatenate([pair_rx[0], pair_rx[1]], axis=0)
    chip_copies = []
    for slot, (dx, dz) in enumerate(CHIPS):
        copy = pltpu.make_async_remote_copy(
            src_ref=chip_rx.at[chip], dst_ref=chip_rx.at[chip],
            send_sem=chip_ss.at[slot], recv_sem=chip_rs.at[slot],
            device_id=chip_peer(dx, dz), device_id_type=pl.DeviceIdType.MESH,
        )
        copy.start()
        chip_copies.append(copy)

    core_copies = []
    for v in range(2):
        shaped(v, other)
        clip_patch = patch[v * CLIP_ROWS : (v + 1) * CLIP_ROWS, :]
        t_send[v] = mm(gh_ref[v, other], clip_patch, TN).astype(jnp.bfloat16)
        copy = pltpu.make_async_remote_copy(
            src_ref=t_send.at[v], dst_ref=t_recv.at[v],
            send_sem=core_ss.at[v], recv_sem=core_rs.at[v],
            device_id=twin, device_id_type=pl.DeviceIdType.MESH,
        )
        copy.start()
        core_copies.append(copy)

    for v in range(2):
        shaped(v, core)
        t_own[v] = mm(gh_ref[v, core], patch[v * CLIP_ROWS : (v + 1) * CLIP_ROWS, :], TN)

    for copy in chip_copies:
        copy.wait()

    blocks = [chip_rx[j] for j in range(CHIP_COUNT)]
    cap_top = blocks[0]
    for block in blocks[1:]:
        cap_top = jnp.maximum(cap_top, block)
    cap_top = jnp.max(cap_top, axis=0, keepdims=True)
    cap_sum = jnp.exp(blocks[0] - cap_top)
    for block in blocks[1:]:
        cap_sum = cap_sum + jnp.exp(block - cap_top)
    cap_lse = cap_top + jnp.log(jnp.sum(cap_sum, axis=0, keepdims=True))
    row = lax.broadcasted_iota(jnp.int32, (4, CAPS), 0)
    col = lax.broadcasted_iota(jnp.int32, (4, CAPS), 1)
    near = chip_rx[chip]
    near_top = jnp.max(near, axis=1, keepdims=True)
    near_exp = jnp.exp(near - near_top)
    by_clip = near_exp / jnp.sum(near_exp, axis=1, keepdims=True)
    by_cap = jnp.exp(near - cap_lse)
    eye = jnp.where(chip * 4 + row == col, 1.0, 0.0)
    grad = (by_clip + by_cap - 2.0 * eye) * (LOSS_SCALE * 0.5 / CAPS * LOGIT_SCALE / WORDS * SCALE)
    parts = three_parts(grad)
    spread = jnp.concatenate(
        [
            jnp.concatenate(
                [jnp.broadcast_to(parts[4 * t + j : 4 * t + j + 1], (BLOCK, CAPS)) for j in range(4)], axis=0
            )
            for t in range(3)
        ],
        axis=1,
    )
    of_half = jnp.concatenate(
        [member[pl.ds(pl.multiple_of(gx * CHUNK + core * BLOCK, BLOCK), BLOCK), :] for gx in range(XS)], axis=0
    )
    wide_coef[...] = mm(jnp.concatenate([of_half, of_half, of_half], axis=1), spread, NT)

    for copy in core_copies:
        copy.wait()

    def combined(dx, dy):
        block = lax.rem(x + dx, XS) * YS + lax.rem(y + dy, YS)
        rows = pl.ds(pl.multiple_of(block * 32, 32), 32)
        part = jnp.zeros((32, DIM), jnp.float32)
        for j in range(4):
            which = core * 2 + j if j < 2 else other * 2 + j - 2
            factor = wide_coef[rows, pl.ds(pl.multiple_of(which * BLOCK, BLOCK), BLOCK)]
            factor = jnp.concatenate([factor] * 4, axis=1)
            source = t_own[j, rows, :] if j < 2 else t_recv[j - 2, rows, :].astype(jnp.float32)
            part = part + factor * source
        return part

    copies1 = []
    for slot, (dx, dy) in enumerate(PLANE):
        snd1[slot] = combined(dx, dy).astype(jnp.bfloat16)
        copy = pltpu.make_async_remote_copy(
            src_ref=snd1.at[slot], dst_ref=rcv1.at[slot],
            send_sem=ss1.at[slot], recv_sem=rs1.at[slot],
            device_id=plane_peer(dx, dy), device_id_type=pl.DeviceIdType.MESH,
        )
        copy.start()
        copies1.append(copy)
    sum1[...] = combined(0, 0)

    coef = added_parts(mm(parts, member[...], NT), 4)
    for j in range(4):
        coef_ref[j] = coef[j : j + 1]
    for v in range(2):
        def scaled(p, _, v=v):
            rows = pl.ds(pl.multiple_of(p * 112, 16), 112)
            for gx in range(XS):
                for h in range(2):
                    lanes = slice(gx * CHUNK + h * BLOCK, gx * CHUNK + (h + 1) * BLOCK)
                    g = gh_ref[v, h, rows, gx * BLOCK : (gx + 1) * BLOCK].astype(jnp.float32)
                    gs_ref[rows, lanes] = (g * coef_ref[core * 2 + v, :, lanes]).astype(jnp.bfloat16)
            return 0

        lax.fori_loop(0, 7, scaled, 0)
        rows = pl.ds(v * CLIP_ROWS, CLIP_ROWS)
        pg_ref[rows, :] = mm(gs_ref[...], text_perm[...], NN).astype(jnp.bfloat16)

    terms = jnp.sum(cap_lse, axis=1, keepdims=True)
    for j, block in enumerate(blocks):
        clip_top = jnp.max(block, axis=1, keepdims=True)
        clip_lse = clip_top + jnp.log(jnp.sum(jnp.exp(block - clip_top), axis=1, keepdims=True))
        matched = jnp.sum(jnp.where(row + 4 * j == col, block, 0.0), axis=1, keepdims=True)
        terms = terms + jnp.sum(clip_lse - 2.0 * matched, axis=0, keepdims=True)
    loss_ref[...] = terms * (0.5 / CAPS)

    for copy in copies1:
        copy.wait()
    summed = sum1[...]
    for slot in range(len(PLANE)):
        summed = summed + rcv1[slot].astype(jnp.float32)
    for m in range(4):
        own2[m] = summed[:, m * BLOCK : (m + 1) * BLOCK]
    for j in range(ZS):
        part = jnp.concatenate([own2[m, pl.ds(j, 4, stride=8), :] for m in range(4)], axis=1)
        own3[j] = part
        snd2[j] = part.astype(jnp.bfloat16)
    copies2 = []
    for i in (4, 3, 5, 2, 6, 1, 7):
        b = lax.rem(z + i, ZS)
        copy = pltpu.make_async_remote_copy(
            src_ref=snd2.at[b], dst_ref=rcv2.at[i - 1],
            send_sem=ss2.at[i - 1], recv_sem=rs2.at[i - 1],
            device_id=far_peer(i), device_id_type=pl.DeviceIdType.MESH,
        )
        copy.start()
        copies2.append(copy)
    result = own3[z]
    for copy in copies2:
        copy.wait()
    for i in range(ZS - 1):
        result = result + rcv2[i].astype(jnp.float32)
    tg_ref[...] = result


def store(loss_in, pg_in, tg_in, loss_out, pg_out, tg_out, sems):
    copies = [
        pltpu.make_async_copy(pg_in, pg_out, sems.at[0]),
        pltpu.make_async_copy(tg_in, tg_out, sems.at[1]),
        pltpu.make_async_copy(loss_in, loss_out, sems.at[2]),
    ]
    for copy in copies:
        copy.start()
    for copy in copies:
        copy.wait()


def fused(text, patches, slots):
    f32, bf16 = jnp.float32, jnp.bfloat16
    vmem = pltpu.VMEM
    dma = pltpu.SemaphoreType.DMA
    shapes = (
        jax.ShapeDtypeStruct((1, 1), f32),
        jax.ShapeDtypeStruct((2 * CLIP_ROWS, DIM), bf16),
        jax.ShapeDtypeStruct((4, DIM), f32),
    )
    results = pl.pallas_call(
        kernel,
        out_shape=shapes,
        in_specs=[pl.BlockSpec(memory_space=pltpu.HBM)] * 3,
        out_specs=(pl.BlockSpec(memory_space=vmem),) * 3,
        scratch_shapes=[
            vmem((ROWS, DIM), bf16),
            vmem((ROWS, DIM), bf16),
            vmem((2 * CLIP_ROWS, DIM), bf16),
            vmem((2, FRAMES), jnp.int32),
            vmem((2, FRAMES, BLOCK), f32),
            vmem((ROWS, CAPS), bf16),
            vmem((8, CLIP_ROWS, CHUNK), f32),
            vmem((2, 2, CLIP_ROWS, HALF), bf16),
            vmem((YS, 2, 2, ROWS), f32),
            vmem((CS, 2, CAPS), f32),
            vmem((CHIP_COUNT, 4, CAPS), f32),
            vmem((2, 2, ROWS), f32),
            vmem((2, HALF, DIM), f32),
            vmem((2, HALF, DIM), bf16),
            vmem((2, HALF, DIM), bf16),
            vmem((4, 1, ROWS), f32),
            vmem((HALF, 4 * BLOCK), f32),
            vmem((15, 32, DIM), bf16),
            vmem((15, 32, DIM), bf16),
            vmem((32, DIM), f32),
            vmem((ZS, 4, DIM), bf16),
            vmem((4, 32, BLOCK), f32),
            vmem((ZS, 4, DIM), f32),
            vmem((ZS - 1, 4, DIM), bf16),
            vmem((CLIP_ROWS, ROWS), bf16),
            dma((4,)), dma((2,)), dma,
            dma((3,)), dma((3,)), dma, dma, dma((31,)), dma((31,)), dma((2,)), dma((2,)),
            dma((15,)), dma((15,)), dma((7,)), dma((7,)),
        ],
        compiler_params=pltpu.CompilerParams(
            collective_id=0, has_side_effects=True, vmem_limit_bytes=44 * 1024 * 1024
        ),
    )(*[pltpu.with_memory_space_constraint(a, pltpu.HBM) for a in (text, patches, slots)])
    return pl.pallas_call(
        store,
        out_shape=shapes,
        in_specs=[pl.BlockSpec(memory_space=pl.ANY)] * 3,
        out_specs=(pl.BlockSpec(memory_space=pl.ANY),) * 3,
        scratch_shapes=[dma((3,))],
    )(*[pltpu.with_memory_space_constraint(a, pltpu.VMEM) for a in results])


def per_device(text, patches, frame_slots):
    flat = patches.transpose(0, 2, 1, 3).reshape(2 * CLIP_ROWS, DIM)
    loss, grad, text_grad = fused(text, flat, frame_slots)
    grad = grad.reshape(2, PATCH, FRAMES, DIM).transpose(0, 2, 1, 3)
    return loss.reshape(()), grad, text_grad


def solution(mesh):
    finer = Mesh(mesh.devices.reshape(XS, ZS, CS, YS), ("x", "z", "core", "y"))
    clip = ("x", "z", "core")
    in_specs = (P(), P(clip, None, "y", None), P(clip, None))
    out_specs = (P(), P(clip, None, "y", None), P((*clip, "y"), None))
    return jax.shard_map(
        per_device, mesh=finer, in_specs=in_specs, out_specs=out_specs, check_vma=False
    )
```

```python
import jax
import jax.numpy as jnp
from jax import lax
from jax.experimental import pallas as pl
from jax.experimental.pallas import tpu as pltpu
from jax.sharding import Mesh
from jax.sharding import PartitionSpec as P

XS, ZS, CS, YS = 4, 8, 2, 4
WORDS = 8
ROWS = 1024
DIM = 512
FRAMES = 16
PATCH = 49
CLIP_ROWS = FRAMES * PATCH
CAPS = 128
CHUNK = 256
HALF = 512
BLOCK = 128
SCALE = DIM**-0.5
LOG2E = 1.4426950408889634
LN2 = 0.6931471805599453
BIG = 1e30
LOGIT_SCALE = 32.0
LOSS_SCALE = 8192.0
CHIP_COUNT = XS * ZS
CHIPS = sorted(
    ((dx, dz) for dx in range(XS) for dz in range(ZS) if dx or dz),
    key=lambda d: (-min(d[0], XS - d[0]) - min(d[1], ZS - d[1]), d),
)
PLANE = sorted(
    ((dx, dy) for dx in range(XS) for dy in range(YS) if dx or dy),
    key=lambda d: (-min(d[0], XS - d[0]) - min(d[1], YS - d[1]), d),
)
NT = (((1,), (1,)), ((), ()))
NN = (((1,), (0,)), ((), ()))
TN = (((0,), (0,)), ((), ()))


def mm(a, b, dims):
    return lax.dot_general(a, b, dims, preferred_element_type=jnp.float32)


def three_parts(value):
    first = value.astype(jnp.bfloat16)
    rest = value - first.astype(jnp.float32)
    second = rest.astype(jnp.bfloat16)
    third = (rest - second.astype(jnp.float32)).astype(jnp.bfloat16)
    return jnp.concatenate([first, second, third], axis=0)


def added_parts(value, rows):
    return value[:rows] + value[rows : 2 * rows] + value[2 * rows : 3 * rows]


def kernel(
    text_hbm, patch_hbm, slots_hbm,
    loss_ref, pg_ref, tg_ref,
    text_in, text_perm, patch, slots_ref, bias_ref, member,
    z_ref, gh_ref, cap_rx, pair_rx, chip_rx, local,
    t_own, t_send, t_recv, coef_ref, wide_coef,
    snd1, rcv1, sum1, snd2, own2, own3, rcv2, gs_ref,
    text_sem, patch_sem, slots_sem,
    cap_ss, cap_rs, pair_ss, pair_rs, chip_ss, chip_rs, core_ss, core_rs,
    ss1, rs1, ss2, rs2,
):
    x = lax.axis_index("x")
    z = lax.axis_index("z")
    core = lax.axis_index("core")
    y = lax.axis_index("y")
    other = 1 - core
    chip = x * ZS + z

    slots_copy = pltpu.make_async_copy(slots_hbm, slots_ref, slots_sem)
    text_copies, patch_copies = [], []

    def fetch_text(n):
        rows = pl.ds(n * CHUNK, CHUNK)
        text_copies.append(pltpu.make_async_copy(text_hbm.at[rows], text_in.at[rows], text_sem.at[n]))
        text_copies[-1].start()

    def fetch_patch(v):
        rows = pl.ds(v * CLIP_ROWS, CLIP_ROWS)
        patch_copies.append(pltpu.make_async_copy(patch_hbm.at[rows], patch.at[rows], patch_sem.at[v]))
        patch_copies[-1].start()

    for n in range(XS):
        fetch_text(n)
    slots_copy.start()

    def far_peer(i):
        return (x, lax.rem(z + i, ZS), core, y)

    def cap_peer(i):
        return (x, z, core, lax.rem(y + i, YS))

    def plane_peer(dx, dy):
        return (lax.rem(x + dx, XS), z, core, lax.rem(y + dy, YS))

    def chip_peer(dx, dz):
        return (lax.rem(x + dx, XS), lax.rem(z + dz, ZS), core, y)

    twin = (x, z, other, y)

    barrier = pltpu.get_barrier_semaphore()
    peers = [chip_peer(dx, dz) for dx, dz in CHIPS]
    peers += [plane_peer(dx, dy) for dx, dy in PLANE if dy]
    peers.append(twin)
    for n, peer in enumerate(peers):
        if n == 24:
            fetch_patch(0)
            fetch_patch(1)
        pl.semaphore_signal(barrier, inc=1, device_id=peer, device_id_type=pl.DeviceIdType.MESH)

    q = lax.broadcasted_iota(jnp.int32, (CHUNK, CHUNK), 0)
    r = lax.broadcasted_iota(jnp.int32, (CHUNK, CHUNK), 1)
    source = (q % 8) * 32 + (q // 32) * 4 + (q // 8) % 4
    order = jnp.where(source == r, 1.0, 0.0).astype(jnp.bfloat16)

    def arrange(gx):
        text_copies[gx].wait()
        rows = slice(gx * CHUNK, (gx + 1) * CHUNK)
        text_perm[rows, :] = mm(order, text_in[rows, :], NN).astype(jnp.bfloat16)

    def tiled(value):
        return jnp.broadcast_to(value, (FRAMES, CHUNK))

    def wide_bias(v):
        part = bias_ref[v]
        return jnp.concatenate([part, part], axis=1)

    def multiply(i):
        v, n = i // 4, i % 4
        z_ref[i] = mm(
            patch[v * CLIP_ROWS : (v + 1) * CLIP_ROWS, :],
            text_perm[n * CHUNK : (n + 1) * CHUNK, :],
            NT,
        )

    def statistics(i):
        v, n = i // 4, i % 4
        top = z_ref[i, 0:FRAMES, :]
        for p in range(1, PATCH):
            top = jnp.maximum(top, z_ref[i, p * FRAMES : (p + 1) * FRAMES, :])
        bias = wide_bias(v)
        peak = jnp.max(top + bias, axis=0, keepdims=True) * (SCALE * LOG2E)
        offset = bias - tiled(peak)
        total = jnp.zeros((FRAMES, CHUNK), jnp.float32)
        weighted = jnp.zeros((FRAMES, CHUNK), jnp.float32)
        for p in range(PATCH):
            s = z_ref[i, p * FRAMES : (p + 1) * FRAMES, :]
            e = jnp.exp2(s * (SCALE * LOG2E) + offset)
            total = total + e
            weighted = weighted + e * s
        total = jnp.sum(total, axis=0, keepdims=True)
        weighted = jnp.sum(weighted, axis=0, keepdims=True)
        lanes = slice(n * CHUNK, (n + 1) * CHUNK)
        local[v, 0:1, lanes] = peak + jnp.log(total) * LOG2E
        local[v, 1:2, lanes] = weighted * SCALE / total

    arrange(0)
    slots_copy.wait()
    slots = slots_ref[...]
    at_row = lax.broadcasted_iota(jnp.int32, (FRAMES, FRAMES), 0)
    at_col = lax.broadcasted_iota(jnp.int32, (FRAMES, FRAMES), 1)
    for v in range(2):
        usable = jnp.where(slots[v : v + 1] >= 0, 0.0, -BIG)
        spread = jnp.where(at_row == at_col, jnp.broadcast_to(usable, (FRAMES, FRAMES)), 0.0)
        column = jnp.sum(spread, axis=1, keepdims=True)
        bias_ref[v] = jnp.broadcast_to(column, (FRAMES, BLOCK))

    for n in range(1, XS):
        arrange(n)
    patch_copies[0].wait()
    patch_copies[1].wait()
    multiply(0)
    for i in range(8):
        if i < 7:
            multiply(i + 1)
        statistics(i)

    cap_rx[y] = local[...]
    pl.semaphore_wait(barrier, len(peers))

    cap_copies = []
    for i in range(1, YS):
        copy = pltpu.make_async_remote_copy(
            src_ref=cap_rx.at[y], dst_ref=cap_rx.at[y],
            send_sem=cap_ss.at[i - 1], recv_sem=cap_rs.at[i - 1],
            device_id=cap_peer(i), device_id_type=pl.DeviceIdType.MESH,
        )
        copy.start()
        cap_copies.append(copy)

    q = lax.broadcasted_iota(jnp.int32, (ROWS, CAPS), 0)
    c = lax.broadcasted_iota(jnp.int32, (ROWS, CAPS), 1)
    qx, qh, qy, qz = q // 256, (q // 128) % 2, (q // 32) % 4, q % 8
    caption = qx * 32 + qz * 4 + qh * 2 + qy // 2
    member[...] = jnp.where(caption == c, 1.0, 0.0).astype(jnp.bfloat16)

    for copy in cap_copies:
        copy.wait_recv()

    lse, pooled = [], []
    for v in range(2):
        parts = [cap_rx[j, v, 0:1, :] for j in range(YS)]
        top = jnp.maximum(jnp.maximum(parts[0], parts[1]), jnp.maximum(parts[2], parts[3]))
        factors = [jnp.exp2(part - top) for part in parts]
        total = factors[0] + factors[1] + factors[2] + factors[3]
        mean = factors[0] * cap_rx[0, v, 1:2, :]
        for j in range(1, YS):
            mean = mean + factors[j] * cap_rx[j, v, 1:2, :]
        pooled.append(mean / total)
        lse.append(top + jnp.log(total) * LOG2E)
    both = jnp.concatenate(pooled, axis=0)
    logits_own = added_parts(mm(three_parts(both), member[...], NN), 2) * (LOGIT_SCALE / WORDS)
    pair_rx[core] = logits_own
    pair_copy = pltpu.make_async_remote_copy(
        src_ref=pair_rx.at[core], dst_ref=pair_rx.at[core],
        send_sem=pair_ss, recv_sem=pair_rs,
        device_id=twin, device_id_type=pl.DeviceIdType.MESH,
    )
    pair_copy.start()

    for copy in cap_copies:
        copy.wait_send()
    for v in range(2):
        cap_rx[y, v, 0:1, :] = lse[v]
        cap_rx[y, v, 1:2, :] = 1.0 - pooled[v]

    def shaped(v, half):
        near = pl.ds(pl.multiple_of(half * BLOCK, BLOCK), BLOCK)
        for n in range(XS):
            lanes = pl.ds(pl.multiple_of(n * CHUNK + half * BLOCK, BLOCK), BLOCK)
            offset = bias_ref[v] - jnp.broadcast_to(cap_rx[y, v, 0:1, lanes], (FRAMES, BLOCK))
            shift = jnp.broadcast_to(cap_rx[y, v, 1:2, lanes], (FRAMES, BLOCK))
            for p in range(PATCH):
                rows = slice(p * FRAMES, (p + 1) * FRAMES)
                s = z_ref[v * 4 + n, rows, near]
                w = jnp.exp2(s * (SCALE * LOG2E) + offset)
                g = w * (s * SCALE + shift)
                gh_ref[v, half, rows, n * BLOCK : (n + 1) * BLOCK] = g.astype(jnp.bfloat16)

    def turned(v, half):
        return mm(gh_ref[v, half], patch[v * CLIP_ROWS : (v + 1) * CLIP_ROWS, :], TN)

    pair_copy.wait_recv()
    chip_rx[chip] = jnp.concatenate([pair_rx[0], pair_rx[1]], axis=0)
    chip_copies = []
    for slot, (dx, dz) in enumerate(CHIPS):
        copy = pltpu.make_async_remote_copy(
            src_ref=chip_rx.at[chip], dst_ref=chip_rx.at[chip],
            send_sem=chip_ss.at[slot], recv_sem=chip_rs.at[slot],
            device_id=chip_peer(dx, dz), device_id_type=pl.DeviceIdType.MESH,
        )
        copy.start()
        chip_copies.append(copy)

    def to_twin(v):
        copy = pltpu.make_async_remote_copy(
            src_ref=t_send.at[v], dst_ref=t_recv.at[v],
            send_sem=core_ss.at[v], recv_sem=core_rs.at[v],
            device_id=twin, device_id_type=pl.DeviceIdType.MESH,
        )
        copy.start()
        return copy

    shaped(0, other)
    t_send[0] = turned(0, other).astype(jnp.bfloat16)
    shaped(1, other)
    core_copies = [to_twin(0)]
    t_send[1] = turned(1, other).astype(jnp.bfloat16)
    shaped(0, core)
    core_copies.append(to_twin(1))
    t_own[0] = turned(0, core)
    shaped(1, core)
    t_own[1] = turned(1, core)

    for copy in chip_copies:
        copy.wait_recv()

    blocks = [chip_rx[j] for j in range(CHIP_COUNT)]
    cap_top = blocks[0]
    for block in blocks[1:]:
        cap_top = jnp.maximum(cap_top, block)
    cap_top = jnp.max(cap_top, axis=0, keepdims=True)
    cap_sum = jnp.exp(blocks[0] - cap_top)
    for block in blocks[1:]:
        cap_sum = cap_sum + jnp.exp(block - cap_top)
    cap_lse = cap_top + jnp.log(jnp.sum(cap_sum, axis=0, keepdims=True))
    row = lax.broadcasted_iota(jnp.int32, (4, CAPS), 0)
    col = lax.broadcasted_iota(jnp.int32, (4, CAPS), 1)
    near = chip_rx[chip]
    near_top = jnp.max(near, axis=1, keepdims=True)
    near_exp = jnp.exp(near - near_top)
    by_clip = near_exp / jnp.sum(near_exp, axis=1, keepdims=True)
    by_cap = jnp.exp(near - cap_lse)
    eye = jnp.where(chip * 4 + row == col, 1.0, 0.0)
    grad = (by_clip + by_cap - 2.0 * eye) * (LOSS_SCALE * 0.5 / CAPS * LOGIT_SCALE / WORDS * SCALE)
    parts = three_parts(grad)
    spread = jnp.concatenate(
        [
            jnp.concatenate(
                [jnp.broadcast_to(parts[4 * t + j : 4 * t + j + 1], (BLOCK, CAPS)) for j in range(4)], axis=0
            )
            for t in range(3)
        ],
        axis=1,
    )
    of_half = jnp.concatenate(
        [member[pl.ds(pl.multiple_of(gx * CHUNK + core * BLOCK, BLOCK), BLOCK), :] for gx in range(XS)], axis=0
    )
    wide_coef[...] = mm(jnp.concatenate([of_half, of_half, of_half], axis=1), spread, NT)

    for copy in core_copies:
        copy.wait_recv()

    def combined(dx, dy):
        block = lax.rem(x + dx, XS) * YS + lax.rem(y + dy, YS)
        rows = pl.ds(pl.multiple_of(block * 32, 32), 32)
        part = jnp.zeros((32, DIM), jnp.float32)
        for j in range(4):
            which = core * 2 + j if j < 2 else other * 2 + j - 2
            factor = wide_coef[rows, pl.ds(pl.multiple_of(which * BLOCK, BLOCK), BLOCK)]
            factor = jnp.concatenate([factor] * 4, axis=1)
            source = t_own[j, rows, :] if j < 2 else t_recv[j - 2, rows, :].astype(jnp.float32)
            part = part + factor * source
        return part

    copies1 = []
    for slot, (dx, dy) in enumerate(PLANE):
        snd1[slot] = combined(dx, dy).astype(jnp.bfloat16)
        copy = pltpu.make_async_remote_copy(
            src_ref=snd1.at[slot], dst_ref=rcv1.at[slot],
            send_sem=ss1.at[slot], recv_sem=rs1.at[slot],
            device_id=plane_peer(dx, dy), device_id_type=pl.DeviceIdType.MESH,
        )
        copy.start()
        copies1.append(copy)
    sum1[...] = combined(0, 0)

    coef = added_parts(mm(parts, member[...], NT), 4)
    for j in range(4):
        coef_ref[j] = coef[j : j + 1]
    for v in range(2):
        def scaled(p, _, v=v):
            rows = pl.ds(pl.multiple_of(p * 112, 16), 112)
            for gx in range(XS):
                for h in range(2):
                    lanes = slice(gx * CHUNK + h * BLOCK, gx * CHUNK + (h + 1) * BLOCK)
                    g = gh_ref[v, h, rows, gx * BLOCK : (gx + 1) * BLOCK].astype(jnp.float32)
                    gs_ref[rows, lanes] = (g * coef_ref[core * 2 + v, :, lanes]).astype(jnp.bfloat16)
            return 0

        lax.fori_loop(0, 7, scaled, 0)
        rows = pl.ds(v * CLIP_ROWS, CLIP_ROWS)
        pg_ref[rows, :] = mm(gs_ref[...], text_perm[...], NN).astype(jnp.bfloat16)

    terms = jnp.sum(cap_lse, axis=1, keepdims=True)
    for j, block in enumerate(blocks):
        clip_top = jnp.max(block, axis=1, keepdims=True)
        clip_lse = clip_top + jnp.log(jnp.sum(jnp.exp(block - clip_top), axis=1, keepdims=True))
        matched = jnp.sum(jnp.where(row + 4 * j == col, block, 0.0), axis=1, keepdims=True)
        terms = terms + jnp.sum(clip_lse - 2.0 * matched, axis=0, keepdims=True)
    loss_ref[...] = terms * (0.5 / CAPS)

    for copy in copies1:
        copy.wait_recv()
    summed = sum1[...]
    for slot in range(len(PLANE)):
        summed = summed + rcv1[slot].astype(jnp.float32)
    for m in range(4):
        own2[m] = summed[:, m * BLOCK : (m + 1) * BLOCK]
    for j in range(ZS):
        part = jnp.concatenate([own2[m, pl.ds(j, 4, stride=8), :] for m in range(4)], axis=1)
        own3[j] = part
        snd2[j] = part.astype(jnp.bfloat16)
    copies2 = []
    for i in (4, 3, 5, 2, 6, 1, 7):
        b = lax.rem(z + i, ZS)
        copy = pltpu.make_async_remote_copy(
            src_ref=snd2.at[b], dst_ref=rcv2.at[i - 1],
            send_sem=ss2.at[i - 1], recv_sem=rs2.at[i - 1],
            device_id=far_peer(i), device_id_type=pl.DeviceIdType.MESH,
        )
        copy.start()
        copies2.append(copy)
    result = own3[z]
    for copy in [pair_copy] + core_copies + chip_copies + copies1:
        copy.wait_send()
    for copy in copies2:
        copy.wait_recv()
    for i in range(ZS - 1):
        result = result + rcv2[i].astype(jnp.float32)
    tg_ref[...] = result
    for copy in copies2:
        copy.wait_send()


def store(loss_in, pg_in, tg_in, loss_out, pg_out, tg_out, sems):
    copies = [
        pltpu.make_async_copy(pg_in, pg_out, sems.at[0]),
        pltpu.make_async_copy(tg_in, tg_out, sems.at[1]),
        pltpu.make_async_copy(loss_in, loss_out, sems.at[2]),
    ]
    for copy in copies:
        copy.start()
    for copy in copies:
        copy.wait()


def fused(text, patches, slots):
    f32, bf16 = jnp.float32, jnp.bfloat16
    vmem = pltpu.VMEM
    dma = pltpu.SemaphoreType.DMA
    shapes = (
        jax.ShapeDtypeStruct((1, 1), f32),
        jax.ShapeDtypeStruct((2 * CLIP_ROWS, DIM), bf16),
        jax.ShapeDtypeStruct((4, DIM), f32),
    )
    results = pl.pallas_call(
        kernel,
        out_shape=shapes,
        in_specs=[pl.BlockSpec(memory_space=pltpu.HBM)] * 3,
        out_specs=(pl.BlockSpec(memory_space=vmem),) * 3,
        scratch_shapes=[
            vmem((ROWS, DIM), bf16),
            vmem((ROWS, DIM), bf16),
            vmem((2 * CLIP_ROWS, DIM), bf16),
            vmem((2, FRAMES), jnp.int32),
            vmem((2, FRAMES, BLOCK), f32),
            vmem((ROWS, CAPS), bf16),
            vmem((8, CLIP_ROWS, CHUNK), f32),
            vmem((2, 2, CLIP_ROWS, HALF), bf16),
            vmem((YS, 2, 2, ROWS), f32),
            vmem((CS, 2, CAPS), f32),
            vmem((CHIP_COUNT, 4, CAPS), f32),
            vmem((2, 2, ROWS), f32),
            vmem((2, HALF, DIM), f32),
            vmem((2, HALF, DIM), bf16),
            vmem((2, HALF, DIM), bf16),
            vmem((4, 1, ROWS), f32),
            vmem((HALF, 4 * BLOCK), f32),
            vmem((15, 32, DIM), bf16),
            vmem((15, 32, DIM), bf16),
            vmem((32, DIM), f32),
            vmem((ZS, 4, DIM), bf16),
            vmem((4, 32, BLOCK), f32),
            vmem((ZS, 4, DIM), f32),
            vmem((ZS - 1, 4, DIM), bf16),
            vmem((CLIP_ROWS, ROWS), bf16),
            dma((4,)), dma((2,)), dma,
            dma((3,)), dma((3,)), dma, dma, dma((31,)), dma((31,)), dma((2,)), dma((2,)),
            dma((15,)), dma((15,)), dma((7,)), dma((7,)),
        ],
        compiler_params=pltpu.CompilerParams(
            collective_id=0, has_side_effects=True, vmem_limit_bytes=44 * 1024 * 1024
        ),
    )(*[pltpu.with_memory_space_constraint(a, pltpu.HBM) for a in (text, patches, slots)])
    return pl.pallas_call(
        store,
        out_shape=shapes,
        in_specs=[pl.BlockSpec(memory_space=pl.ANY)] * 3,
        out_specs=(pl.BlockSpec(memory_space=pl.ANY),) * 3,
        scratch_shapes=[dma((3,))],
    )(*[pltpu.with_memory_space_constraint(a, pltpu.VMEM) for a in results])


def per_device(text, patches, frame_slots):
    flat = patches.transpose(0, 2, 1, 3).reshape(2 * CLIP_ROWS, DIM)
    loss, grad, text_grad = fused(text, flat, frame_slots)
    grad = grad.reshape(2, PATCH, FRAMES, DIM).transpose(0, 2, 1, 3)
    return loss.reshape(()), grad, text_grad


def solution(mesh):
    finer = Mesh(mesh.devices.reshape(XS, ZS, CS, YS), ("x", "z", "core", "y"))
    clip = ("x", "z", "core")
    in_specs = (P(), P(clip, None, "y", None), P(clip, None))
    out_specs = (P(), P(clip, None, "y", None), P((*clip, "y"), None))
    return jax.shard_map(
        per_device, mesh=finer, in_specs=in_specs, out_specs=out_specs, check_vma=False
    )
```

```python
import jax
import jax.numpy as jnp
from jax import lax
from jax.experimental import pallas as pl
from jax.experimental.pallas import tpu as pltpu
from jax.sharding import Mesh
from jax.sharding import PartitionSpec as P

XS, ZS, CS, YS = 4, 8, 2, 4
WORDS = 8
ROWS = 1024
DIM = 512
FRAMES = 16
PATCH = 49
CLIP_ROWS = FRAMES * PATCH
CAPS = 128
CHUNK = 256
HALF = 512
BLOCK = 128
SCALE = DIM**-0.5
LOG2E = 1.4426950408889634
LN2 = 0.6931471805599453
BIG = 1e30
LOGIT_SCALE = 32.0
LOSS_SCALE = 8192.0
CHIP_COUNT = XS * ZS
CHIPS = sorted(
    ((dx, dz) for dx in range(XS) for dz in range(ZS) if dx or dz),
    key=lambda d: (-min(d[0], XS - d[0]) - min(d[1], ZS - d[1]), d),
)
PLANE = sorted(
    ((dx, dy) for dx in range(XS) for dy in range(YS) if dx or dy),
    key=lambda d: (-min(d[0], XS - d[0]) - min(d[1], YS - d[1]), d),
)
NT = (((1,), (1,)), ((), ()))
NN = (((1,), (0,)), ((), ()))
TN = (((0,), (0,)), ((), ()))


def mm(a, b, dims):
    return lax.dot_general(a, b, dims, preferred_element_type=jnp.float32)


def three_parts(value):
    first = value.astype(jnp.bfloat16)
    rest = value - first.astype(jnp.float32)
    second = rest.astype(jnp.bfloat16)
    third = (rest - second.astype(jnp.float32)).astype(jnp.bfloat16)
    return jnp.concatenate([first, second, third], axis=0)


def added_parts(value, rows):
    return value[:rows] + value[rows : 2 * rows] + value[2 * rows : 3 * rows]


def kernel(
    text_hbm, patch_hbm, slots_hbm,
    loss_ref, pg_ref, tg_ref,
    text_in, text_perm, patch, slots_ref, bias_ref, member,
    z_ref, gh_ref, cap_rx, pair_rx, chip_rx, local,
    t_own, t_send, t_recv, coef_ref, wide_coef,
    snd1, rcv1, sum1, snd2, own2, own3, rcv2, gs_ref,
    text_sem, patch_sem, slots_sem,
    cap_ss, cap_rs, pair_ss, pair_rs, chip_ss, chip_rs, core_ss, core_rs,
    ss1, rs1, ss2, rs2,
):
    x = lax.axis_index("x")
    z = lax.axis_index("z")
    core = lax.axis_index("core")
    y = lax.axis_index("y")
    other = 1 - core
    chip = x * ZS + z

    slots_copy = pltpu.make_async_copy(slots_hbm, slots_ref, slots_sem)
    text_copies, patch_copies = [], []

    def fetch_text(n):
        rows = pl.ds(n * CHUNK, CHUNK)
        text_copies.append(pltpu.make_async_copy(text_hbm.at[rows], text_in.at[rows], text_sem.at[n]))
        text_copies[-1].start()

    def fetch_patch(v):
        rows = pl.ds(v * CLIP_ROWS, CLIP_ROWS)
        patch_copies.append(pltpu.make_async_copy(patch_hbm.at[rows], patch.at[rows], patch_sem.at[v]))
        patch_copies[-1].start()

    for n in range(XS):
        fetch_text(n)
    slots_copy.start()

    def far_peer(i):
        return (x, lax.rem(z + i, ZS), core, y)

    def cap_peer(i):
        return (x, z, core, lax.rem(y + i, YS))

    def plane_peer(dx, dy):
        return (lax.rem(x + dx, XS), z, core, lax.rem(y + dy, YS))

    def chip_peer(dx, dz):
        return (lax.rem(x + dx, XS), lax.rem(z + dz, ZS), core, y)

    twin = (x, z, other, y)

    barrier = pltpu.get_barrier_semaphore()
    peers = [chip_peer(dx, dz) for dx, dz in CHIPS]
    peers += [plane_peer(dx, dy) for dx, dy in PLANE if dy]
    peers.append(twin)
    for n, peer in enumerate(peers):
        if n == 24:
            fetch_patch(0)
            fetch_patch(1)
        pl.semaphore_signal(barrier, inc=1, device_id=peer, device_id_type=pl.DeviceIdType.MESH)

    q = lax.broadcasted_iota(jnp.int32, (CHUNK, CHUNK), 0)
    r = lax.broadcasted_iota(jnp.int32, (CHUNK, CHUNK), 1)
    source = (q % 8) * 32 + (q // 32) * 4 + (q // 8) % 4
    order = jnp.where(source == r, 1.0, 0.0).astype(jnp.bfloat16)

    def arrange(gx):
        text_copies[gx].wait()
        rows = slice(gx * CHUNK, (gx + 1) * CHUNK)
        text_perm[rows, :] = mm(order, text_in[rows, :], NN).astype(jnp.bfloat16)

    def tiled(value):
        return jnp.broadcast_to(value, (FRAMES, CHUNK))

    def wide_bias(v):
        part = bias_ref[v]
        return jnp.concatenate([part, part], axis=1)

    def multiply(i):
        v, n = i // 4, i % 4
        z_ref[i] = mm(
            patch[v * CLIP_ROWS : (v + 1) * CLIP_ROWS, :],
            text_perm[n * CHUNK : (n + 1) * CHUNK, :],
            NT,
        )

    def statistics(i):
        v, n = i // 4, i % 4
        top = z_ref[i, 0:FRAMES, :]
        for p in range(1, PATCH):
            top = jnp.maximum(top, z_ref[i, p * FRAMES : (p + 1) * FRAMES, :])
        bias = wide_bias(v)
        peak = jnp.max(top + bias, axis=0, keepdims=True) * (SCALE * LOG2E)
        offset = bias - tiled(peak)
        total = jnp.zeros((FRAMES, CHUNK), jnp.float32)
        weighted = jnp.zeros((FRAMES, CHUNK), jnp.float32)
        for p in range(PATCH):
            s = z_ref[i, p * FRAMES : (p + 1) * FRAMES, :]
            e = jnp.exp2(s * (SCALE * LOG2E) + offset)
            total = total + e
            weighted = weighted + e * s
        total = jnp.sum(total, axis=0, keepdims=True)
        weighted = jnp.sum(weighted, axis=0, keepdims=True)
        lanes = slice(n * CHUNK, (n + 1) * CHUNK)
        local[v, 0:1, lanes] = peak + jnp.log(total) * LOG2E
        local[v, 1:2, lanes] = weighted * SCALE / total

    arrange(0)
    slots_copy.wait()
    slots = slots_ref[...]
    at_row = lax.broadcasted_iota(jnp.int32, (FRAMES, FRAMES), 0)
    at_col = lax.broadcasted_iota(jnp.int32, (FRAMES, FRAMES), 1)
    for v in range(2):
        usable = jnp.where(slots[v : v + 1] >= 0, 0.0, -BIG)
        spread = jnp.where(at_row == at_col, jnp.broadcast_to(usable, (FRAMES, FRAMES)), 0.0)
        column = jnp.sum(spread, axis=1, keepdims=True)
        bias_ref[v] = jnp.broadcast_to(column, (FRAMES, BLOCK))

    for n in range(1, XS):
        arrange(n)
    patch_copies[0].wait()
    patch_copies[1].wait()
    multiply(0)
    for i in range(8):
        if i < 7:
            multiply(i + 1)
        statistics(i)

    cap_rx[y] = local[...]
    pl.semaphore_wait(barrier, len(peers))

    cap_copies = []
    for i in range(1, YS):
        copy = pltpu.make_async_remote_copy(
            src_ref=cap_rx.at[y], dst_ref=cap_rx.at[y],
            send_sem=cap_ss.at[i - 1], recv_sem=cap_rs.at[i - 1],
            device_id=cap_peer(i), device_id_type=pl.DeviceIdType.MESH,
        )
        copy.start()
        cap_copies.append(copy)

    q = lax.broadcasted_iota(jnp.int32, (ROWS, CAPS), 0)
    c = lax.broadcasted_iota(jnp.int32, (ROWS, CAPS), 1)
    qx, qh, qy, qz = q // 256, (q // 128) % 2, (q // 32) % 4, q % 8
    caption = qx * 32 + qz * 4 + qh * 2 + qy // 2
    member[...] = jnp.where(caption == c, 1.0, 0.0).astype(jnp.bfloat16)

    for copy in cap_copies:
        copy.wait_recv()

    lse, pooled = [], []
    for v in range(2):
        parts = [cap_rx[j, v, 0:1, :] for j in range(YS)]
        top = jnp.maximum(jnp.maximum(parts[0], parts[1]), jnp.maximum(parts[2], parts[3]))
        factors = [jnp.exp2(part - top) for part in parts]
        total = factors[0] + factors[1] + factors[2] + factors[3]
        mean = factors[0] * cap_rx[0, v, 1:2, :]
        for j in range(1, YS):
            mean = mean + factors[j] * cap_rx[j, v, 1:2, :]
        pooled.append(mean / total)
        lse.append(top + jnp.log(total) * LOG2E)
    both = jnp.concatenate(pooled, axis=0)
    logits_own = added_parts(mm(three_parts(both), member[...], NN), 2) * (LOGIT_SCALE / WORDS)
    pair_rx[core] = logits_own
    pair_copy = pltpu.make_async_remote_copy(
        src_ref=pair_rx.at[core], dst_ref=pair_rx.at[core],
        send_sem=pair_ss, recv_sem=pair_rs,
        device_id=twin, device_id_type=pl.DeviceIdType.MESH,
    )
    pair_copy.start()

    for copy in cap_copies:
        copy.wait_send()
    for v in range(2):
        cap_rx[y, v, 0:1, :] = lse[v]
        cap_rx[y, v, 1:2, :] = 1.0 - pooled[v]

    def shaped(v, half):
        near = pl.ds(pl.multiple_of(half * BLOCK, BLOCK), BLOCK)
        for n in range(XS):
            lanes = pl.ds(pl.multiple_of(n * CHUNK + half * BLOCK, BLOCK), BLOCK)
            offset = bias_ref[v] - jnp.broadcast_to(cap_rx[y, v, 0:1, lanes], (FRAMES, BLOCK))
            shift = jnp.broadcast_to(cap_rx[y, v, 1:2, lanes], (FRAMES, BLOCK))
            for p in range(PATCH):
                rows = slice(p * FRAMES, (p + 1) * FRAMES)
                s = z_ref[v * 4 + n, rows, near]
                w = jnp.exp2(s * (SCALE * LOG2E) + offset)
                g = w * (s * SCALE + shift)
                gh_ref[v, half, rows, n * BLOCK : (n + 1) * BLOCK] = g.astype(jnp.bfloat16)

    def turned(v, half):
        return mm(gh_ref[v, half], patch[v * CLIP_ROWS : (v + 1) * CLIP_ROWS, :], TN)

    pair_copy.wait_recv()
    chip_rx[chip] = jnp.concatenate([pair_rx[0], pair_rx[1]], axis=0)
    chip_copies = []
    for slot, (dx, dz) in enumerate(CHIPS):
        copy = pltpu.make_async_remote_copy(
            src_ref=chip_rx.at[chip], dst_ref=chip_rx.at[chip],
            send_sem=chip_ss.at[slot], recv_sem=chip_rs.at[slot],
            device_id=chip_peer(dx, dz), device_id_type=pl.DeviceIdType.MESH,
        )
        copy.start()
        chip_copies.append(copy)

    def to_twin(v):
        copy = pltpu.make_async_remote_copy(
            src_ref=t_send.at[v], dst_ref=t_recv.at[v],
            send_sem=core_ss.at[v], recv_sem=core_rs.at[v],
            device_id=twin, device_id_type=pl.DeviceIdType.MESH,
        )
        copy.start()
        return copy

    shaped(0, other)
    t_send[0] = turned(0, other).astype(jnp.bfloat16)
    shaped(1, other)
    core_copies = [to_twin(0)]
    t_send[1] = turned(1, other).astype(jnp.bfloat16)
    shaped(0, core)
    core_copies.append(to_twin(1))
    t_own[0] = turned(0, core)
    shaped(1, core)
    t_own[1] = turned(1, core)

    for copy in chip_copies:
        copy.wait_recv()

    blocks = [chip_rx[j] for j in range(CHIP_COUNT)]
    cap_top = blocks[0]
    for block in blocks[1:]:
        cap_top = jnp.maximum(cap_top, block)
    cap_top = jnp.max(cap_top, axis=0, keepdims=True)
    cap_sum = jnp.exp(blocks[0] - cap_top)
    for block in blocks[1:]:
        cap_sum = cap_sum + jnp.exp(block - cap_top)
    cap_lse = cap_top + jnp.log(jnp.sum(cap_sum, axis=0, keepdims=True))
    row = lax.broadcasted_iota(jnp.int32, (4, CAPS), 0)
    col = lax.broadcasted_iota(jnp.int32, (4, CAPS), 1)
    near = chip_rx[chip]
    near_top = jnp.max(near, axis=1, keepdims=True)
    near_exp = jnp.exp(near - near_top)
    by_clip = near_exp / jnp.sum(near_exp, axis=1, keepdims=True)
    by_cap = jnp.exp(near - cap_lse)
    eye = jnp.where(chip * 4 + row == col, 1.0, 0.0)
    grad = (by_clip + by_cap - 2.0 * eye) * (LOSS_SCALE * 0.5 / CAPS * LOGIT_SCALE / WORDS * SCALE)
    parts = three_parts(grad)
    spread = jnp.concatenate(
        [
            jnp.concatenate(
                [jnp.broadcast_to(parts[4 * t + j : 4 * t + j + 1], (BLOCK, CAPS)) for j in range(4)], axis=0
            )
            for t in range(3)
        ],
        axis=1,
    )
    of_half = jnp.concatenate(
        [member[pl.ds(pl.multiple_of(gx * CHUNK + core * BLOCK, BLOCK), BLOCK), :] for gx in range(XS)], axis=0
    )
    wide_coef[...] = mm(jnp.concatenate([of_half, of_half, of_half], axis=1), spread, NT)

    for copy in core_copies:
        copy.wait_recv()

    def combined(dx, dy):
        block = lax.rem(x + dx, XS) * YS + lax.rem(y + dy, YS)
        rows = pl.ds(pl.multiple_of(block * 32, 32), 32)
        part = jnp.zeros((32, DIM), jnp.float32)
        for j in range(4):
            which = core * 2 + j if j < 2 else other * 2 + j - 2
            factor = wide_coef[rows, pl.ds(pl.multiple_of(which * BLOCK, BLOCK), BLOCK)]
            factor = jnp.concatenate([factor] * 4, axis=1)
            source = t_own[j, rows, :] if j < 2 else t_recv[j - 2, rows, :].astype(jnp.float32)
            part = part + factor * source
        return part

    copies1 = []
    for slot, (dx, dy) in enumerate(PLANE):
        snd1[slot] = combined(dx, dy).astype(jnp.bfloat16)
        copy = pltpu.make_async_remote_copy(
            src_ref=snd1.at[slot], dst_ref=rcv1.at[slot],
            send_sem=ss1.at[slot], recv_sem=rs1.at[slot],
            device_id=plane_peer(dx, dy), device_id_type=pl.DeviceIdType.MESH,
        )
        copy.start()
        copies1.append(copy)
    sum1[...] = combined(0, 0)

    coef = added_parts(mm(parts, member[...], NT), 4)
    for j in range(4):
        coef_ref[j] = coef[j : j + 1]
    for v in range(2):
        def scaled(p, _, v=v):
            rows = pl.ds(pl.multiple_of(p * 112, 16), 112)
            for gx in range(XS):
                for h in range(2):
                    lanes = slice(gx * CHUNK + h * BLOCK, gx * CHUNK + (h + 1) * BLOCK)
                    g = gh_ref[v, h, rows, gx * BLOCK : (gx + 1) * BLOCK].astype(jnp.float32)
                    gs_ref[rows, lanes] = (g * coef_ref[core * 2 + v, :, lanes]).astype(jnp.bfloat16)
            return 0

        lax.fori_loop(0, 7, scaled, 0)
        rows = pl.ds(v * CLIP_ROWS, CLIP_ROWS)
        pg_ref[rows, :] = mm(gs_ref[...], text_perm[...], NN).astype(jnp.bfloat16)

    terms = jnp.sum(cap_lse, axis=1, keepdims=True)
    for j, block in enumerate(blocks):
        clip_top = jnp.max(block, axis=1, keepdims=True)
        clip_lse = clip_top + jnp.log(jnp.sum(jnp.exp(block - clip_top), axis=1, keepdims=True))
        matched = jnp.sum(jnp.where(row + 4 * j == col, block, 0.0), axis=1, keepdims=True)
        terms = terms + jnp.sum(clip_lse - 2.0 * matched, axis=0, keepdims=True)
    loss_ref[...] = terms * (0.5 / CAPS)

    summed = sum1[...]
    for slot, copy in enumerate(copies1):
        copy.wait_recv()
        summed = summed + rcv1[slot].astype(jnp.float32)
    for m in range(4):
        own2[m] = summed[:, m * BLOCK : (m + 1) * BLOCK]
    for j in range(ZS):
        part = jnp.concatenate([own2[m, pl.ds(j, 4, stride=8), :] for m in range(4)], axis=1)
        own3[j] = part
        snd2[j] = part.astype(jnp.bfloat16)
    copies2 = []
    for i in (4, 3, 5, 2, 6, 1, 7):
        b = lax.rem(z + i, ZS)
        copy = pltpu.make_async_remote_copy(
            src_ref=snd2.at[b], dst_ref=rcv2.at[i - 1],
            send_sem=ss2.at[i - 1], recv_sem=rs2.at[i - 1],
            device_id=far_peer(i), device_id_type=pl.DeviceIdType.MESH,
        )
        copy.start()
        copies2.append(copy)
    result = own3[z]
    for copy in [pair_copy] + core_copies + chip_copies + copies1:
        copy.wait_send()
    for i, copy in zip((4, 3, 5, 2, 6, 1, 7), copies2):
        copy.wait_recv()
        result = result + rcv2[i - 1].astype(jnp.float32)
    tg_ref[...] = result
    for copy in copies2:
        copy.wait_send()


def store(loss_in, pg_in, tg_in, loss_out, pg_out, tg_out, sems):
    copies = [
        pltpu.make_async_copy(pg_in, pg_out, sems.at[0]),
        pltpu.make_async_copy(tg_in, tg_out, sems.at[1]),
        pltpu.make_async_copy(loss_in, loss_out, sems.at[2]),
    ]
    for copy in copies:
        copy.start()
    for copy in copies:
        copy.wait()


def fused(text, patches, slots):
    f32, bf16 = jnp.float32, jnp.bfloat16
    vmem = pltpu.VMEM
    dma = pltpu.SemaphoreType.DMA
    shapes = (
        jax.ShapeDtypeStruct((1, 1), f32),
        jax.ShapeDtypeStruct((2 * CLIP_ROWS, DIM), bf16),
        jax.ShapeDtypeStruct((4, DIM), f32),
    )
    results = pl.pallas_call(
        kernel,
        out_shape=shapes,
        in_specs=[pl.BlockSpec(memory_space=pltpu.HBM)] * 3,
        out_specs=(pl.BlockSpec(memory_space=vmem),) * 3,
        scratch_shapes=[
            vmem((ROWS, DIM), bf16),
            vmem((ROWS, DIM), bf16),
            vmem((2 * CLIP_ROWS, DIM), bf16),
            vmem((2, FRAMES), jnp.int32),
            vmem((2, FRAMES, BLOCK), f32),
            vmem((ROWS, CAPS), bf16),
            vmem((8, CLIP_ROWS, CHUNK), f32),
            vmem((2, 2, CLIP_ROWS, HALF), bf16),
            vmem((YS, 2, 2, ROWS), f32),
            vmem((CS, 2, CAPS), f32),
            vmem((CHIP_COUNT, 4, CAPS), f32),
            vmem((2, 2, ROWS), f32),
            vmem((2, HALF, DIM), f32),
            vmem((2, HALF, DIM), bf16),
            vmem((2, HALF, DIM), bf16),
            vmem((4, 1, ROWS), f32),
            vmem((HALF, 4 * BLOCK), f32),
            vmem((15, 32, DIM), bf16),
            vmem((15, 32, DIM), bf16),
            vmem((32, DIM), f32),
            vmem((ZS, 4, DIM), bf16),
            vmem((4, 32, BLOCK), f32),
            vmem((ZS, 4, DIM), f32),
            vmem((ZS - 1, 4, DIM), bf16),
            vmem((CLIP_ROWS, ROWS), bf16),
            dma((4,)), dma((2,)), dma,
            dma((3,)), dma((3,)), dma, dma, dma((31,)), dma((31,)), dma((2,)), dma((2,)),
            dma((15,)), dma((15,)), dma((7,)), dma((7,)),
        ],
        compiler_params=pltpu.CompilerParams(
            collective_id=0, has_side_effects=True, vmem_limit_bytes=44 * 1024 * 1024
        ),
    )(*[pltpu.with_memory_space_constraint(a, pltpu.HBM) for a in (text, patches, slots)])
    return pl.pallas_call(
        store,
        out_shape=shapes,
        in_specs=[pl.BlockSpec(memory_space=pl.ANY)] * 3,
        out_specs=(pl.BlockSpec(memory_space=pl.ANY),) * 3,
        scratch_shapes=[dma((3,))],
    )(*[pltpu.with_memory_space_constraint(a, pltpu.VMEM) for a in results])


def per_device(text, patches, frame_slots):
    flat = patches.transpose(0, 2, 1, 3).reshape(2 * CLIP_ROWS, DIM)
    loss, grad, text_grad = fused(text, flat, frame_slots)
    grad = grad.reshape(2, PATCH, FRAMES, DIM).transpose(0, 2, 1, 3)
    return loss.reshape(()), grad, text_grad


def solution(mesh):
    finer = Mesh(mesh.devices.reshape(XS, ZS, CS, YS), ("x", "z", "core", "y"))
    clip = ("x", "z", "core")
    in_specs = (P(), P(clip, None, "y", None), P(clip, None))
    out_specs = (P(), P(clip, None, "y", None), P((*clip, "y"), None))
    return jax.shard_map(
        per_device, mesh=finer, in_specs=in_specs, out_specs=out_specs, check_vma=False
    )
```
